32 devices in a mesh: grp: 2 (over y), seq: 4 (over z), chan: 2 (over x), sub: 2 (over core).
Axes of the slice: x: 2, y: 2, z: 4, core: 2. Of those that a mesh axis runs over, the one named last changes fastest.
Arguments:
- tokens: bfloat16 [2048, 4096], P(('grp', 'seq'), ('chan', 'sub')), parts along dimension 0, may hold values from -6 to 6
- tangent: bfloat16 [2048, 4096], P(('grp', 'seq'), ('chan', 'sub')), parts along dimension 0, may hold values from -6 to 6
- in_weight: bfloat16 [4096, 3, 4096], P('seq', None, ('chan', 'sub')), may hold values from -0.09375 to 0.09375
- short_weight: float32 [3, 3, 4096], P(None, None, ('chan', 'sub')), may hold values from -3.5 to 3.5
- long_filter: float32 [1024, 4096], P('seq', ('chan', 'sub')), may hold values from -0.1875 to 0.1875
- skip_gain: float32 [4096], P(('chan', 'sub')), may hold values from 0.5 to 1.5
Outputs:
- output: float32 [2048, 4096], P(('grp', 'seq'), ('chan', 'sub')), parts along dimension 0
- output_tangent: float32 [2048, 4096], P(('grp', 'seq'), ('chan', 'sub')), parts along dimension 0
The draws below stay inside these ranges and needn't reach their ends.
There are 2 independent parts, one for each index of `grp`. The reference program is written for one: setup_inputs(seed, part) draws one part's arguments, and reference() takes and returns one part's arrays. A program takes and returns all parts, laid end to end along the dimension named above; an argument that names none is the same for every part. Nothing has to cross between parts.
All inputs are finite; a program needn't handle non-finite values.
Results may differ from the reference program's by a relative error of at most 0.0003.
Values may be sent and summed in bfloat16 or wider, within the bound.
A program may use at most 128 MiB of HBM per device.

```python
import jax
import jax.numpy as jnp

D = 4096
TAPS = 3
SEQLEN = 1024


def block_scale(own_key, shape, shards, least, high):
    factor_of, own = 1.0, jax.random.fold_in(own_key, 6)
    for position, blocks in shards:
        heights = jnp.exp(jax.random.uniform(jax.random.fold_in(own, position), (blocks,), jnp.float32, least / len(shards), high / len(shards)))
        factor_of = factor_of * jnp.repeat(heights, shape[position] // blocks).reshape([-1 if axis == position else 1 for axis in range(len(shape))])
    return factor_of


def normal_values(rng, dims, deviation, most, cuts=(), kind=jnp.bfloat16):
    array = jax.random.normal(rng, dims, jnp.float32) * deviation
    if len(cuts) > 0:
        array = block_scale(rng, dims, cuts, -0.22, 0.18) * array
    return jnp.clip(array, min=-most, max=most).astype(kind)


def setup_inputs(seed: int = 0, part: int = 0) -> dict:
    key_of = jax.random.split(jax.random.key(seed), 7)
    own_keys = jax.random.split(jax.random.fold_in(key_of[6], part), 7)
    tokens = normal_values(own_keys[0], (SEQLEN, D), 1.0, 6.0, ((0, 4), (1, 4)))
    tangent = normal_values(own_keys[1], (SEQLEN, D), 1.0, 6.0, ((0, 4), (1, 4)))
    in_weight = normal_values(key_of[2], (D, 3, D), D ** -0.5, 0.09375, ((0, 4), (2, 4)))
    short_weight = normal_values(key_of[3], (TAPS, 3, D), TAPS ** -0.5, 3.5, ((2, 4),), jnp.float32)
    long_filter = normal_values(key_of[4], (SEQLEN, D), SEQLEN ** -0.5, 0.1875, ((0, 4), (1, 4)), jnp.float32)
    skip_gain = jnp.clip(0.5 + 1.0 * jax.random.uniform(key_of[5], (D,), jnp.float32) ** block_scale(key_of[5], (D,), ((0, 4),), -0.2, 0.2), 0.5, 1.5)
    return dict(tokens=tokens, tangent=tangent, in_weight=in_weight, short_weight=short_weight, long_filter=long_filter, skip_gain=skip_gain)


def short_filter(projected, short_weight):
    taps = short_weight.shape[0]
    count = projected.shape[0]
    padded = jnp.pad(projected, ((taps - 1, 0), (0, 0), (0, 0)))
    total = jnp.zeros_like(projected)
    for offset in range(taps):
        total = total + short_weight[offset] * padded[taps - 1 - offset: taps - 1 - offset + count]
    return total


def causal_conv(values, spectrum, count):
    size = 2 * count
    return jnp.fft.irfft(jnp.fft.rfft(values, n=size, axis=0) * spectrum, n=size, axis=0)[:count]


def reference(tokens, tangent, in_weight, short_weight, long_filter, skip_gain):
    count, width = tokens.shape
    flat_weight = in_weight.reshape(width, 3 * width)
    proj = jnp.dot(tokens, flat_weight, preferred_element_type=jnp.float32).reshape(count, 3, width)
    dproj = jnp.dot(tangent, flat_weight, preferred_element_type=jnp.float32).reshape(count, 3, width)
    mixed = short_filter(proj, short_weight)
    dmixed = short_filter(dproj, short_weight)
    gated_in = mixed[:, 0, :] * mixed[:, 2, :]
    dgated_in = dmixed[:, 0, :] * mixed[:, 2, :] + mixed[:, 0, :] * dmixed[:, 2, :]
    spectrum = jnp.fft.rfft(long_filter, n=2 * count, axis=0)
    long_conv = causal_conv(gated_in, spectrum, count)
    dlong_conv = causal_conv(dgated_in, spectrum, count)
    combined = long_conv + skip_gain * gated_in
    dcombined = dlong_conv + skip_gain * dgated_in
    output = mixed[:, 1, :] * combined
    output_tangent = dmixed[:, 1, :] * combined + mixed[:, 1, :] * dcombined
    return (output, output_tangent)
```

```python
import functools
import math

import jax
import jax.numpy as jnp
import numpy as np
from jax import lax
from jax.experimental import pallas as pl
from jax.experimental.pallas import tpu as pltpu
from jax.sharding import PartitionSpec as P

HIGH = lax.Precision.HIGH


def dft_table(block):
    size = 2 * block
    freqs = np.arange(block)[:, None]
    times = np.arange(block)[None, :]
    theta = (freqs * times % size) * (2.0 * math.pi / size)
    cosine = np.cos(theta)
    sine = -np.sin(theta)
    sine[0] = 1.0 - 2.0 * (np.arange(block) % 2)
    return np.concatenate([cosine, sine], axis=0).astype(np.float32)


def causal_convs(signals, long_filter, block):
    count = long_filter.shape[0]
    blocks = count // block
    table = jnp.asarray(dft_table(block))
    index = lax.broadcasted_iota(jnp.int32, (block, 1), 0)
    first = index == 0
    sign = (1 - 2 * (index % 2)).astype(jnp.float32)
    weight = jnp.where(first, 0.5 / block, 1.0 / block).astype(jnp.float32)

    def spectra(values):
        result = []
        for b in range(blocks):
            both = jnp.dot(table, values[b * block : (b + 1) * block], precision=HIGH)
            result.append((both[:block], both[block:]))
        return result

    plain = spectra(long_filter)
    kernels = [plain[0]]
    for b in range(1, blocks):
        kernels.append(tuple(here + sign * before for here, before in zip(plain[b], plain[b - 1])))
    outs = []
    for values in signals:
        moved = spectra(values)
        rows = []
        for b in range(blocks):
            real, imag = 0.0, 0.0
            for a in range(b + 1):
                kr, ki = kernels[b - a]
                vr, vi = moved[a]
                rr, ii = kr * vr, ki * vi
                real = real + jnp.where(first, rr, rr - ii)
                imag = imag + jnp.where(first, ii, kr * vi + ki * vr)
            packed = jnp.concatenate([real * weight, imag * weight], axis=0)
            rows.append(
                lax.dot_general(table, packed, (((0,), (0,)), ((), ())), precision=HIGH)
            )
        outs.append(jnp.concatenate(rows, axis=0))
    return outs


def short_filter(values, weights):
    count = values.shape[0]
    total = weights[0] * values
    for offset in range(1, weights.shape[0]):
        total = total + weights[offset] * jnp.pad(values, ((offset, 0), (0, 0)))[:count]
    return total


def operator(proj, dproj, short_weight, long_filter, skip_gain, block):
    mixed = [short_filter(proj[j], short_weight[:, j]) for j in range(3)]
    dmixed = [short_filter(dproj[j], short_weight[:, j]) for j in range(3)]
    gated_in = mixed[0] * mixed[2]
    dgated_in = dmixed[0] * mixed[2] + mixed[0] * dmixed[2]
    conv, dconv = causal_convs((gated_in, dgated_in), long_filter, block)
    combined = conv + skip_gain * gated_in
    dcombined = dconv + skip_gain * dgated_in
    return mixed[1] * combined, dmixed[1] * combined + mixed[1] * dcombined

MESH = pl.DeviceIdType.MESH
DIRECTIONS = (1, -1)


def gather_kernel(
    n, tok, tan, wt, filt, p0, p1, p2, ffull, full, wfull, local_sem,
    col_send, col_recv, x_send, x_recv, c_send, c_recv,
    w_send, w_recv, y_send, y_recv, f_send, f_recv, fy_send, fy_recv,
):
    g, z = lax.axis_index("grp"), lax.axis_index("seq")
    x, c = lax.axis_index("chan"), lax.axis_index("sub")
    rows, wide = tok.shape
    deep, own = wt.shape[1], wt.shape[2] // n
    half, fhalf = deep // 2, filt.shape[0] // 2
    sources = (tok, tan)
    pending = []

    def valid(place):
        return jnp.logical_and(place >= 0, place < n)

    def slot(k, zb, xb, cb):
        top = pl.multiple_of(zb * rows, rows)
        left = pl.multiple_of((xb * 2 + cb) * wide, wide)
        return full.at[k, pl.ds(top, rows), pl.ds(left, wide)]

    def send(src, dst, send_sem, recv_sem, where):
        return pltpu.make_async_remote_copy(
            src_ref=src, dst_ref=dst, send_sem=send_sem, recv_sem=recv_sem,
            device_id=where, device_id_type=MESH,
        )

    def column(k, zb, way, first):
        dst = slot(k, zb, x, c)
        src = sources[k] if first else dst
        lane = 0 if way > 0 else 1
        return send(src, dst, col_send.at[k, zb, lane], col_recv.at[k, zb], {"seq": z + way})

    def across(k, zb, first):
        dst = slot(k, zb, x, c)
        src = sources[k] if first else dst
        return send(src, dst, x_send.at[k, zb], x_recv.at[k, zb], {"chan": 1 - x})

    def sibling(k, zb, other, first):
        xb = 1 - x if other else x
        dst = slot(k, zb, xb, c)
        src = sources[k] if first else dst
        return send(src, dst, c_send.at[k, xb, zb], c_recv.at[k, xb, zb], {"sub": 1 - c})

    def from_sibling(k, zb, xb):
        dst = slot(k, zb, xb, 1 - c)
        return send(dst, dst, c_send.at[k, xb, zb], c_recv.at[k, xb, zb], {"sub": 1 - c})

    def from_across(k, zb):
        dst = slot(k, zb, 1 - x, c)
        return send(dst, dst, x_send.at[k, zb], x_recv.at[k, zb], {"chan": 1 - x})

    def weight_part(j, zb, gb):
        top = pl.multiple_of(zb * deep + gb * half, half)
        return wfull.at[j, pl.ds(top, half), :]

    def filter_part(zb, gb):
        top = pl.multiple_of(zb * 2 * fhalf + gb * fhalf, fhalf)
        return ffull.at[pl.ds(top, fhalf), :]

    def give_weight(j, target):
        left = pl.multiple_of(target * own, own)
        top = pl.multiple_of(g * half, half)
        src = wt.at[j, pl.ds(top, half), pl.ds(left, own)]
        return send(
            src, weight_part(j, z, g), w_send.at[j, target], w_recv.at[j, z], {"seq": target}
        )

    def give_filter(target):
        left = pl.multiple_of(target * own, own)
        top = pl.multiple_of(g * fhalf, fhalf)
        src = filt.at[pl.ds(top, fhalf), pl.ds(left, own)]
        return send(src, filter_part(z, g), f_send.at[target], f_recv.at[z], {"seq": target})

    def take_weight(j, zb):
        ref = weight_part(j, zb, g)
        return send(ref, ref, w_send.at[j, zb], w_recv.at[j, zb], {"seq": zb})

    def take_filter(zb):
        ref = filter_part(zb, g)
        return send(ref, ref, f_send.at[zb], f_recv.at[zb], {"seq": zb})

    def pass_weight(j, zb):
        ref = weight_part(j, zb, g)
        return send(ref, ref, y_send.at[j, zb], y_recv.at[j, zb], {"grp": 1 - g})

    def pass_filter(zb):
        ref = filter_part(zb, g)
        return send(ref, ref, fy_send.at[zb], fy_recv.at[zb], {"grp": 1 - g})

    def end_weight(j, zb):
        ref = weight_part(j, zb, 1 - g)
        return send(ref, ref, y_send.at[j, zb], y_recv.at[j, zb], {"grp": 1 - g})

    def end_filter(zb):
        ref = filter_part(zb, 1 - g)
        return send(ref, ref, fy_send.at[zb], fy_recv.at[zb], {"grp": 1 - g})

    barrier = pltpu.get_barrier_semaphore()
    for d in range(1, n):
        for way in DIRECTIONS:
            there = z + way * d

            @pl.when(valid(there))
            def _():
                pl.semaphore_signal(barrier, inc=1, device_id={"seq": there}, device_id_type=MESH)

    for where in ({"chan": 1 - x}, {"grp": 1 - g}, {"sub": 1 - c}):
        pl.semaphore_signal(barrier, inc=1, device_id=where, device_id_type=MESH)
    pl.semaphore_wait(barrier, n + 2)

    def launch(make, condition=None):
        pending.append((make, condition))
        if condition is None:
            make().start()
        else:
            pl.when(condition)(lambda: make().start())

    for k in range(2):
        for way in DIRECTIONS:
            launch(functools.partial(column, k, z, way, True), valid(z + way))
        launch(functools.partial(across, k, z, True))
        launch(functools.partial(sibling, k, z, False, True))
    mine = pl.ds(pl.multiple_of(z * own, own), own)
    locals_ = [
        pltpu.make_async_copy(tok, slot(0, z, x, c), local_sem.at[0]),
        pltpu.make_async_copy(tan, slot(1, z, x, c), local_sem.at[1]),
        pltpu.make_async_copy(
            wt.at[:, :, mine],
            wfull.at[:, pl.ds(pl.multiple_of(z * deep, deep), deep), :],
            local_sem.at[2],
        ),
        pltpu.make_async_copy(
            filt.at[:, mine],
            ffull.at[pl.ds(pl.multiple_of(z * 2 * fhalf, 2 * fhalf), 2 * fhalf), :],
            local_sem.at[3],
        ),
    ]
    for copy in locals_:
        copy.start()

    def relay_across(d):
        for k in range(2):
            for way in DIRECTIONS[: 1 if d == 0 else 2]:
                zb = z - way * d

                def step(k=k, zb=zb):
                    from_across(k, zb).wait_recv()
                    sibling(k, zb, True, False).start()

                pending.append((functools.partial(sibling, k, zb, True, False), valid(zb)))
                pl.when(valid(zb))(step)

    def relay_column(d):
        for k in range(2):
            for way in DIRECTIONS:
                zb = z - way * d
                on = jnp.logical_and(valid(zb), valid(z + way))

                def arrive(k=k, zb=zb, way=way):
                    column(k, zb, way, False).wait_recv()

                def after(k=k, zb=zb):
                    across(k, zb, False).start()
                    sibling(k, zb, False, False).start()

                pl.when(valid(zb))(arrive)
                launch(functools.partial(column, k, zb, way, False), on)
                pl.when(valid(zb))(after)
                pending.append((functools.partial(across, k, zb, False), valid(zb)))
                pending.append((functools.partial(sibling, k, zb, False, False), valid(zb)))

    def issue(make):
        for d in range(1, n):
            for way in DIRECTIONS:
                launch(functools.partial(make, z + way * d), valid(z + way * d))

    def each_source(step):
        for d in range(1, n):
            for way in DIRECTIONS:
                pl.when(valid(z - way * d))(functools.partial(step, z - way * d))

    def relay(take, give_on):
        def move(zb):
            take(zb).wait_recv()
            give_on(zb).start()

        each_source(move)
        for d in range(1, n):
            for way in DIRECTIONS:
                pending.append((functools.partial(give_on, z - way * d), valid(z - way * d)))

    def issue_weight(j):
        issue(functools.partial(give_weight, j))

    def relay_weight(j):
        relay(functools.partial(take_weight, j), functools.partial(pass_weight, j))

    def finish_weight(j):
        each_source(lambda zb: end_weight(j, zb).wait_recv())

    def finish_tokens(d):
        for way in DIRECTIONS[: 1 if d == 0 else 2]:
            zb = z - way * d

            def finish(zb=zb):
                for k in range(2):
                    for xb in (x, 1 - x):
                        from_sibling(k, zb, xb).wait_recv()

            pl.when(valid(zb))(finish)

    def multiply(j, distances):
        out = (p0, p1, p2)[j]
        for d in distances:
            for way in DIRECTIONS[: 1 if d == 0 else 2]:
                zb = z - way * d

                def product(zb=zb):
                    @pl.loop(0, 2)
                    def _(k):
                        top = pl.multiple_of(zb * rows, rows)
                        to = pl.multiple_of(k * rows * n + zb * rows, rows)
                        out[pl.ds(to, rows), :] = jnp.dot(
                            full[k, pl.ds(top, rows), :], wfull[j],
                            preferred_element_type=jnp.float32,
                        )

                pl.when(valid(zb))(product)

    relay_column(1)
    issue_weight(0)
    relay_across(0)
    for d in range(2, n - 1):
        relay_column(d)
        if d == 2:
            issue_weight(1)
        relay_across(d - 1)
    relay_weight(0)
    issue_weight(2)
    issue(give_filter)
    relay_column(n - 1)
    relay_across(n - 2)
    relay_weight(1)
    relay_across(n - 1)
    for copy in locals_:
        copy.wait()
    finish_weight(0)
    for d in range(n - 1):
        finish_tokens(d)
    multiply(0, range(n - 1))
    relay_weight(2)
    relay(take_filter, pass_filter)
    finish_tokens(n - 1)
    multiply(0, [n - 1])
    finish_weight(1)
    multiply(1, range(n))
    finish_weight(2)
    multiply(2, range(n))
    each_source(lambda zb: end_filter(zb).wait_recv())
    for make, condition in pending:
        if condition is None:
            make().wait_send()
        else:
            pl.when(condition)(lambda make=make: make().wait_send())


def gather_by_copies(tokens, tangent, wt, long_filter):
    n = lax.axis_size("seq")
    rows, wide = tokens.shape
    own = wt.shape[2] // n
    anywhere = pl.BlockSpec(memory_space=pl.ANY)
    sem = pltpu.SemaphoreType.DMA
    return pl.pallas_call(
        functools.partial(gather_kernel, n),
        out_shape=(
            jax.ShapeDtypeStruct((2 * rows * n, own), jnp.float32),
            jax.ShapeDtypeStruct((2 * rows * n, own), jnp.float32),
            jax.ShapeDtypeStruct((2 * rows * n, own), jnp.float32),
            jax.ShapeDtypeStruct((long_filter.shape[0] * n, own), long_filter.dtype),
        ),
        in_specs=[anywhere] * 4,
        out_specs=(pl.BlockSpec(memory_space=pltpu.VMEM),) * 3 + (anywhere,),
        scratch_shapes=[
            pltpu.VMEM((2, rows * n, wide * 4), tokens.dtype),
            pltpu.VMEM((3, wt.shape[1] * n, own), wt.dtype),
            sem((4,)),
            sem((2, n, 2)), sem((2, n)), sem((2, n)), sem((2, n)), sem((2, 2, n)), sem((2, 2, n)),
            sem((3, n)), sem((3, n)), sem((3, n)), sem((3, n)), sem((n,)), sem((n,)), sem((n,)), sem((n,)),
        ],
        compiler_params=pltpu.CompilerParams(collective_id=0, has_side_effects=True, vmem_limit_bytes=48 * 2**20),
        name="gather",
    )(tokens, tangent, wt, long_filter)


def split_table(table, axis):
    high = table.astype(jnp.bfloat16)
    low = (table - high.astype(np.float32)).astype(jnp.bfloat16)
    return np.concatenate([high, high, low], axis=axis)


def split_value(value):
    high = value.astype(jnp.bfloat16)
    return high, (value - high.astype(jnp.float32)).astype(jnp.bfloat16)


TILE = 256
STRIP = 64
POWER = 12
REACH = 1400.0
TINY = 1e-34


def encode(value):
    second = value * value
    fourth = second * second
    code = fourth * fourth * fourth
    return jnp.where(value < 0, -code, code).astype(jnp.bfloat16)


def decode(code, peak):
    value = code.astype(jnp.float32)
    size = jnp.exp2(jnp.log2(jnp.abs(value)) * (1.0 / POWER)) * (peak * (1.0 / REACH))
    return jnp.where(value < 0, -size, size)


def conv_kernel(
    n, block, p0, p1, p2, filt, sw, skip, table, inverse, out0, out1, peaks,
    gates, mids, xin, spec, plain, kern, ycat, conv, raw, res, top_of, send_sem, recv_sem, local_sem,
    peak_send, peak_recv, peak_local,
):
    z = lax.axis_index("seq")
    count = filt.shape[0]
    rows = count // n
    own = filt.shape[1]
    half = own // 2
    blocks = count // block
    outs = (out0, out1)

    def valid(place):
        return jnp.logical_and(place >= 0, place < n)

    barrier = pltpu.get_barrier_semaphore()
    others = [(d, way) for d in range(1, n) for way in DIRECTIONS]
    for d, way in others:
        there = z + way * d

        @pl.when(valid(there))
        def _():
            pl.semaphore_signal(barrier, inc=1, device_id={"seq": there}, device_id_type=MESH)

    pl.semaphore_wait(barrier, n - 1)

    line = lax.broadcasted_iota(jnp.int32, (count, half), 0)

    def forward(value, dst):
        high, low = split_value(value)
        xin[pl.ds(0, block), :] = high
        xin[pl.ds(block, block), :] = low
        xin[pl.ds(2 * block, block), :] = high

        @pl.loop(0, 2 * block // TILE)
        def _(m):
            at = pl.ds(pl.multiple_of(m * TILE, TILE), TILE)
            dst[at, :] = jnp.dot(table[at, :], xin[...], preferred_element_type=jnp.float32)

    def give(h, o, target):
        top = pl.multiple_of(target * rows, rows)
        left = pl.multiple_of(z * own + h * half, half)
        return pltpu.make_async_remote_copy(
            src_ref=res.at[h, o, pl.ds(top, rows), :],
            dst_ref=outs[o].at[:, pl.ds(left, half)],
            send_sem=send_sem.at[h, o, target], recv_sem=recv_sem.at[h, o, z],
            device_id={"seq": target}, device_id_type=MESH,
        )

    def take(h, o, source):
        top = pl.multiple_of(source * rows, rows)
        left = pl.multiple_of(source * own + h * half, half)
        return pltpu.make_async_remote_copy(
            src_ref=res.at[h, o, pl.ds(top, rows), :],
            dst_ref=outs[o].at[:, pl.ds(left, half)],
            send_sem=send_sem.at[h, o, source], recv_sem=recv_sem.at[h, o, source],
            device_id={"seq": source}, device_id_type=MESH,
        )

    def give_peak(h, target):
        left = pl.multiple_of(z * own + h * half, half)
        return pltpu.make_async_remote_copy(
            src_ref=top_of.at[h, target], dst_ref=peaks.at[:, pl.ds(left, half)],
            send_sem=peak_send.at[h, target], recv_sem=peak_recv.at[h, z],
            device_id={"seq": target}, device_id_type=MESH,
        )

    def take_peak(h, source):
        left = pl.multiple_of(source * own + h * half, half)
        return pltpu.make_async_remote_copy(
            src_ref=top_of.at[h, source], dst_ref=peaks.at[:, pl.ds(left, half)],
            send_sem=peak_send.at[h, source], recv_sem=peak_recv.at[h, source],
            device_id={"seq": source}, device_id_type=MESH,
        )

    def keep_peak(h):
        left = pl.multiple_of(z * own + h * half, half)
        return pltpu.make_async_copy(
            top_of.at[h, z], peaks.at[:, pl.ds(left, half)], peak_local.at[h]
        )

    def keep(h, o):
        top = pl.multiple_of(z * rows, rows)
        left = pl.multiple_of(z * own + h * half, half)
        return pltpu.make_async_copy(
            res.at[h, o, pl.ds(top, rows), :], outs[o].at[:, pl.ds(left, half)],
            local_sem.at[h, o],
        )

    for h in range(2):
        lanes = pl.ds(h * half, half)
        taps = sw.shape[0] // 3

        def filtered(ref, j, s):
            value = ref[pl.ds(s * count, count), lanes]
            total = sw[pl.ds(j, 1), lanes] * value
            for o in range(1, taps):
                moved = jnp.where(line >= o, pltpu.roll(value, o, 0), 0.0)
                total = total + sw[pl.ds(o * 3 + j, 1), lanes] * moved
            return total

        first_gate, second_gate = filtered(p0, 0, 0), filtered(p2, 2, 0)
        gates[:, :half] = first_gate * second_gate
        gates[:, half:] = filtered(p0, 0, 1) * second_gate + first_gate * filtered(p2, 2, 1)
        mids[:, :half] = filtered(p1, 1, 0)
        mids[:, half:] = filtered(p1, 1, 1)

        for pair in range(blocks // 2):
            forward(
                jnp.concatenate(
                    [
                        filt[pl.ds(2 * pair * block, block), lanes],
                        filt[pl.ds((2 * pair + 1) * block, block), lanes],
                    ],
                    axis=1,
                ),
                plain.at[pair],
            )
        for b in range(blocks):
            forward(gates[pl.ds(b * block, block), :], spec.at[b])

        @pl.loop(0, 2 * block // STRIP)
        def _(m):
            at = pl.ds(pl.multiple_of(m * STRIP, STRIP), STRIP)
            row = lax.broadcasted_iota(jnp.int32, (STRIP, half), 0)
            sign = (1 - 2 * (row % 2)).astype(jnp.float32)
            before = None
            for b in range(blocks):
                left = (b % 2) * half
                here = plain[b // 2, at, left : left + half]
                mixed = here if before is None else here + sign * before
                kern[b, at, :half] = mixed
                kern[b, at, half:] = mixed
                before = here

        for b in range(blocks):

            @pl.loop(0, block // STRIP)
            def _(m):
                at = pl.ds(pl.multiple_of(m * STRIP, STRIP), STRIP)
                after = pl.ds(pl.multiple_of(block + m * STRIP, STRIP), STRIP)
                row = lax.broadcasted_iota(jnp.int32, (STRIP, 2 * half), 0) + m * STRIP
                first = row == 0
                weight = jnp.where(first, 0.5 / block, 1.0 / block)
                real, imag = 0.0, 0.0
                for a in range(b + 1):
                    kr, ki = kern[b - a, at, :], kern[b - a, after, :]
                    vr, vi = spec[a, at, :], spec[a, after, :]
                    rr, ii = kr * vr, ki * vi
                    real = real + jnp.where(first, rr, rr - ii)
                    imag = imag + jnp.where(first, ii, kr * vi + ki * vr)
                for base, value in ((0, real), (block, imag)):
                    high, low = split_value(value * weight)
                    for third, part in enumerate((high, low, high)):
                        start = pl.multiple_of(third * 2 * block + base + m * STRIP, STRIP)
                        ycat[pl.ds(start, STRIP), :] = part

            @pl.loop(0, block // TILE)
            def _(m):
                at = pl.ds(pl.multiple_of(m * TILE, TILE), TILE)
                to = pl.ds(pl.multiple_of(b * block + m * TILE, TILE), TILE)
                conv[to, :] = jnp.dot(
                    inverse[at, :], ycat[...], preferred_element_type=jnp.float32
                )

        @pl.loop(0, n)
        def _(target):
            gain = skip[:, lanes]

            def values(m, most):
                at = pl.ds(pl.multiple_of(target * rows + m * STRIP, STRIP), STRIP)
                combined = conv[at, :half] + gain * gates[at, :half]
                dcombined = conv[at, half:] + gain * gates[at, half:]
                middle = mids[at, :half]
                first = middle * combined
                second = mids[at, half:] * combined + middle * dcombined
                raw[0, at, :] = first
                raw[1, at, :] = second
                return tuple(
                    jnp.maximum(old, jnp.max(jnp.abs(new).reshape(STRIP // 8, 8, half), axis=0))
                    for old, new in zip(most, (first, second))
                )

            nothing = jnp.zeros((8, half), jnp.float32)
            most = lax.fori_loop(0, rows // STRIP, values, (nothing, nothing))
            for o in range(2):
                peak = jnp.maximum(jnp.max(most[o], axis=0, keepdims=True), TINY)
                top_of[h, target, pl.ds(8 * o, 8), :] = jnp.broadcast_to(peak, (8, half))
                scale = REACH / peak

                @pl.loop(0, rows // STRIP)
                def _(m):
                    at = pl.ds(pl.multiple_of(target * rows + m * STRIP, STRIP), STRIP)
                    res[h, o, at, :] = encode(raw[o, at, :] * scale)

        for d, way in reversed(others):
            target = z + way * d

            def send_all(h=h, target=target):
                give_peak(h, target).start()
                for o in range(2):
                    give(h, o, target).start()

            pl.when(valid(target))(send_all)
        keep_peak(h).start()
        for o in range(2):
            keep(h, o).start()

    for h in range(2):
        keep_peak(h).wait()
        for o in range(2):
            keep(h, o).wait()
        for d, way in others:
            there = z + way * d

            def finish(h=h, there=there):
                take_peak(h, there).wait_recv()
                give_peak(h, there).wait_send()
                for o in range(2):
                    take(h, o, there).wait_recv()
                    give(h, o, there).wait_send()

            pl.when(valid(there))(finish)


def convolve_and_return(projs, long_filter, short_weight, skip_gain, block):
    n = lax.axis_size("seq")
    count, own = long_filter.shape
    blocks = count // block
    table = dft_table(block)
    vmem = pl.BlockSpec(memory_space=pltpu.VMEM)
    anywhere = pl.BlockSpec(memory_space=pl.ANY)
    sem = pltpu.SemaphoreType.DMA
    shape = jax.ShapeDtypeStruct((count // n, own * n), jnp.bfloat16)
    f32, bf16 = jnp.float32, jnp.bfloat16
    first, second, peaks = pl.pallas_call(
        functools.partial(conv_kernel, n, block),
        out_shape=(shape, shape, jax.ShapeDtypeStruct((16, own * n), f32)),
        in_specs=[vmem] * 8,
        out_specs=(anywhere, anywhere, anywhere),
        scratch_shapes=[
            pltpu.VMEM((count, own), f32),
            pltpu.VMEM((count, own), f32),
            pltpu.VMEM((3 * block, own), bf16),
            pltpu.VMEM((blocks, 2 * block, own), f32),
            pltpu.VMEM((blocks // 2, 2 * block, own), f32),
            pltpu.VMEM((blocks, 2 * block, own), f32),
            pltpu.VMEM((6 * block, own), bf16),
            pltpu.VMEM((count, own), f32),
            pltpu.VMEM((2, count, own // 2), f32),
            pltpu.VMEM((2, 2, count, own // 2), bf16),
            pltpu.VMEM((2, n, 16, own // 2), f32),
            sem((2, 2, n)), sem((2, 2, n)), sem((2, 2)),
            sem((2, n)), sem((2, n)), sem((2,)),
        ],
        compiler_params=pltpu.CompilerParams(
            collective_id=1, has_side_effects=True, vmem_limit_bytes=48 * 2**20
        ),
        name="convolve",
    )(
        *projs, long_filter, short_weight.reshape(-1, own), skip_gain.reshape(1, own),
        jnp.asarray(split_table(table, 1)), jnp.asarray(split_table(table.T, 1)),
    )
    return decode(first, peaks[0:1]), decode(second, peaks[8:9])


def body(tokens, tangent, in_weight, short_weight, long_filter, skip_gain):
    devices = lax.axis_size("seq")
    shard = lax.axis_index("seq")
    own = in_weight.shape[2] // devices
    wt = in_weight.transpose(1, 0, 2)
    by_copies = own == 256 and devices == 4 and all(lax.axis_size(axis) == 2 for axis in ("grp", "chan", "sub"))
    if by_copies:
        *projs, long_filter = gather_by_copies(tokens, tangent, wt, long_filter)
    else:
        both = jnp.stack([tokens, tangent])
        both = lax.all_gather(both, ("chan", "sub"), axis=2, tiled=True)
        both = lax.all_gather(both, "seq", axis=1, tiled=True)
        weight = lax.all_to_all(wt, "seq", split_axis=2, concat_axis=1, tiled=True)
        long_filter = lax.all_to_all(long_filter, "seq", split_axis=1, concat_axis=0, tiled=True)
    short_weight = lax.dynamic_slice_in_dim(short_weight, shard * own, own, axis=2)
    skip_gain = lax.dynamic_slice_in_dim(skip_gain, shard * own, own, axis=0)

    block = min(512, long_filter.shape[0])
    if by_copies:
        return convolve_and_return(projs, long_filter, short_weight, skip_gain, block)

    def project(values):
        return [jnp.dot(values, weight[j], preferred_element_type=jnp.float32) for j in range(3)]

    proj, dproj = project(both[0]), project(both[1])
    outs = operator(proj, dproj, short_weight, long_filter, skip_gain, block)
    return tuple(
        lax.all_to_all(value, "seq", split_axis=0, concat_axis=1, tiled=True) for value in outs
    )


def solution(mesh):
    placed = (
        P(("grp", "seq"), ("chan", "sub")),
        P(("grp", "seq"), ("chan", "sub")),
        P("seq", None, ("chan", "sub")),
        P(None, None, ("chan", "sub")),
        P("seq", ("chan", "sub")),
        P(("chan", "sub")),
    )
    return jax.shard_map(
        body,
        mesh=mesh,
        in_specs=placed,
        out_specs=(P(("grp", "seq"), ("chan", "sub")), P(("grp", "seq"), ("chan", "sub"))),
        check_vma=False,
    )
```

```python
import functools
import math

import jax
import jax.numpy as jnp
import numpy as np
from jax import lax
from jax.experimental import pallas as pl
from jax.experimental.pallas import tpu as pltpu
from jax.sharding import PartitionSpec as P

HIGH = lax.Precision.HIGH


def dft_table(block):
    size = 2 * block
    freqs = np.arange(block)[:, None]
    times = np.arange(block)[None, :]
    theta = (freqs * times % size) * (2.0 * math.pi / size)
    cosine = np.cos(theta)
    sine = -np.sin(theta)
    sine[0] = 1.0 - 2.0 * (np.arange(block) % 2)
    return np.concatenate([cosine, sine], axis=0).astype(np.float32)


def causal_convs(signals, long_filter, block):
    count = long_filter.shape[0]
    blocks = count // block
    table = jnp.asarray(dft_table(block))
    index = lax.broadcasted_iota(jnp.int32, (block, 1), 0)
    first = index == 0
    sign = (1 - 2 * (index % 2)).astype(jnp.float32)
    weight = jnp.where(first, 0.5 / block, 1.0 / block).astype(jnp.float32)

    def spectra(values):
        result = []
        for b in range(blocks):
            both = jnp.dot(table, values[b * block : (b + 1) * block], precision=HIGH)
            result.append((both[:block], both[block:]))
        return result

    plain = spectra(long_filter)
    kernels = [plain[0]]
    for b in range(1, blocks):
        kernels.append(tuple(here + sign * before for here, before in zip(plain[b], plain[b - 1])))
    outs = []
    for values in signals:
        moved = spectra(values)
        rows = []
        for b in range(blocks):
            real, imag = 0.0, 0.0
            for a in range(b + 1):
                kr, ki = kernels[b - a]
                vr, vi = moved[a]
                rr, ii = kr * vr, ki * vi
                real = real + jnp.where(first, rr, rr - ii)
                imag = imag + jnp.where(first, ii, kr * vi + ki * vr)
            packed = jnp.concatenate([real * weight, imag * weight], axis=0)
            rows.append(
                lax.dot_general(table, packed, (((0,), (0,)), ((), ())), precision=HIGH)
            )
        outs.append(jnp.concatenate(rows, axis=0))
    return outs


def short_filter(values, weights):
    count = values.shape[0]
    total = weights[0] * values
    for offset in range(1, weights.shape[0]):
        total = total + weights[offset] * jnp.pad(values, ((offset, 0), (0, 0)))[:count]
    return total


def operator(proj, dproj, short_weight, long_filter, skip_gain, block):
    mixed = [short_filter(proj[j], short_weight[:, j]) for j in range(3)]
    dmixed = [short_filter(dproj[j], short_weight[:, j]) for j in range(3)]
    gated_in = mixed[0] * mixed[2]
    dgated_in = dmixed[0] * mixed[2] + mixed[0] * dmixed[2]
    conv, dconv = causal_convs((gated_in, dgated_in), long_filter, block)
    combined = conv + skip_gain * gated_in
    dcombined = dconv + skip_gain * dgated_in
    return mixed[1] * combined, dmixed[1] * combined + mixed[1] * dcombined

MESH = pl.DeviceIdType.MESH
DIRECTIONS = (1, -1)


def split_table(table, axis):
    high = table.astype(jnp.bfloat16)
    low = (table - high.astype(np.float32)).astype(jnp.bfloat16)
    return np.concatenate([high, high, low], axis=axis)


def split_value(value):
    high = value.astype(jnp.bfloat16)
    return high, (value - high.astype(jnp.float32)).astype(jnp.bfloat16)


TILE = 256
STRIP = 64
POWER = 12
REACH = 1400.0
TINY = 1e-34


def encode(value):
    second = value * value
    fourth = second * second
    code = fourth * fourth * fourth
    return jnp.where(value < 0, -code, code).astype(jnp.bfloat16)


def decode(code, peak):
    value = code.astype(jnp.float32)
    size = jnp.exp2(jnp.log2(jnp.abs(value)) * (1.0 / POWER)) * (peak * (1.0 / REACH))
    return jnp.where(value < 0, -size, size)


def hyena_kernel(
    n, block, tok, tan, wt, filt, sw, skip, table_in, inverse_in, out0, out1, peaks,
    full, pairs, mid, ffull, table, inverse, p02, p1,
    gates, mids, xin, spec, plain, kern, ycat, conv, raw, res, top_of,
    local_sem, own_sem, col_send, col_recv, x_send, x_recv, c_send, c_recv,
    w_send, w_recv, y_send, y_recv, f_send, f_recv, fy_send, fy_recv,
    send_sem, recv_sem, keep_sem, peak_send, peak_recv, peak_keep,
):
    g, z = lax.axis_index("grp"), lax.axis_index("seq")
    x, c = lax.axis_index("chan"), lax.axis_index("sub")
    rows, wide = tok.shape
    count = rows * n
    deep, own = wt.shape[1], wt.shape[2] // n
    half, deep2, fhalf = own // 2, deep // 2, filt.shape[0] // 2
    blocks = count // block
    taps = sw.shape[0]
    sources = (tok, tan)
    outs = (out0, out1)
    pending = []

    def valid(place):
        return jnp.logical_and(place >= 0, place < n)

    def send(src, dst, send_sem, recv_sem, where):
        return pltpu.make_async_remote_copy(
            src_ref=src, dst_ref=dst, send_sem=send_sem, recv_sem=recv_sem,
            device_id=where, device_id_type=MESH,
        )

    def slot(k, zb, xb, cb):
        top = pl.multiple_of(zb * rows, rows)
        left = pl.multiple_of((xb * 2 + cb) * wide, wide)
        return full.at[k, pl.ds(top, rows), pl.ds(left, wide)]

    def column(k, zb, way, first):
        dst = slot(k, zb, x, c)
        src = sources[k] if first else dst
        lane = 0 if way > 0 else 1
        return send(src, dst, col_send.at[k, zb, lane], col_recv.at[k, zb], {"seq": z + way})

    def across(k, zb, first):
        dst = slot(k, zb, x, c)
        src = sources[k] if first else dst
        return send(src, dst, x_send.at[k, zb], x_recv.at[k, zb], {"chan": 1 - x})

    def sibling(k, zb, other, first):
        xb = 1 - x if other else x
        dst = slot(k, zb, xb, c)
        src = sources[k] if first else dst
        return send(src, dst, c_send.at[k, xb, zb], c_recv.at[k, xb, zb], {"sub": 1 - c})

    def from_sibling(k, zb, xb):
        dst = slot(k, zb, xb, 1 - c)
        return send(dst, dst, c_send.at[k, xb, zb], c_recv.at[k, xb, zb], {"sub": 1 - c})

    def from_across(k, zb):
        dst = slot(k, zb, 1 - x, c)
        return send(dst, dst, x_send.at[k, zb], x_recv.at[k, zb], {"chan": 1 - x})

    def weight_rows(piece, top, size):
        j, h = piece
        if j == 1:
            return mid.at[pl.ds(top, size), pl.ds(h * half, half)]
        return pairs.at[h, pl.ds(top, size), pl.ds((j // 2) * half, half)]

    def weight_part(piece, zb, gb):
        return weight_rows(piece, pl.multiple_of(zb * deep + gb * deep2, deep2), deep2)

    def filter_part(zb, gb):
        top = pl.multiple_of(zb * 2 * fhalf + gb * fhalf, fhalf)
        return ffull.at[pl.ds(top, fhalf), :]

    def number(piece):
        return piece[0] * 2 + piece[1]

    def give_weight(piece, target):
        left = pl.multiple_of(target * own + piece[1] * half, half)
        top = pl.multiple_of(g * deep2, deep2)
        src = wt.at[piece[0], pl.ds(top, deep2), pl.ds(left, half)]
        q = number(piece)
        return send(
            src, weight_part(piece, z, g), w_send.at[q, target], w_recv.at[q, z], {"seq": target}
        )

    def give_filter(target):
        left = pl.multiple_of(target * own, own)
        top = pl.multiple_of(g * fhalf, fhalf)
        src = filt.at[pl.ds(top, fhalf), pl.ds(left, own)]
        return send(src, filter_part(z, g), f_send.at[target], f_recv.at[z], {"seq": target})

    def take_weight(piece, zb):
        ref, q = weight_part(piece, zb, g), number(piece)
        return send(ref, ref, w_send.at[q, zb], w_recv.at[q, zb], {"seq": zb})

    def take_filter(zb):
        ref = filter_part(zb, g)
        return send(ref, ref, f_send.at[zb], f_recv.at[zb], {"seq": zb})

    def pass_weight(piece, zb):
        ref, q = weight_part(piece, zb, g), number(piece)
        return send(ref, ref, y_send.at[q, zb], y_recv.at[q, zb], {"grp": 1 - g})

    def pass_filter(zb):
        ref = filter_part(zb, g)
        return send(ref, ref, fy_send.at[zb], fy_recv.at[zb], {"grp": 1 - g})

    def end_weight(piece, zb):
        ref, q = weight_part(piece, zb, 1 - g), number(piece)
        return send(ref, ref, y_send.at[q, zb], y_recv.at[q, zb], {"grp": 1 - g})

    def end_filter(zb):
        ref = filter_part(zb, 1 - g)
        return send(ref, ref, fy_send.at[zb], fy_recv.at[zb], {"grp": 1 - g})

    barrier = pltpu.get_barrier_semaphore()
    for d in range(1, n):
        for way in DIRECTIONS:
            there = z + way * d

            @pl.when(valid(there))
            def _():
                pl.semaphore_signal(barrier, inc=1, device_id={"seq": there}, device_id_type=MESH)

    for where in ({"chan": 1 - x}, {"grp": 1 - g}, {"sub": 1 - c}):
        pl.semaphore_signal(barrier, inc=1, device_id=where, device_id_type=MESH)
    pl.semaphore_wait(barrier, n + 2)

    def launch(make, condition=None):
        pending.append((make, condition))
        if condition is None:
            make().start()
        else:
            pl.when(condition)(lambda: make().start())

    for k in range(2):
        for way in DIRECTIONS:
            launch(functools.partial(column, k, z, way, True), valid(z + way))
        launch(functools.partial(across, k, z, True))
        launch(functools.partial(sibling, k, z, False, True))
    mine = pl.ds(pl.multiple_of(z * own, own), own)
    locals_ = [
        pltpu.make_async_copy(tok, slot(0, z, x, c), local_sem.at[0]),
        pltpu.make_async_copy(tan, slot(1, z, x, c), local_sem.at[1]),
        pltpu.make_async_copy(
            filt.at[:, mine],
            ffull.at[pl.ds(pl.multiple_of(z * 2 * fhalf, 2 * fhalf), 2 * fhalf), :],
            local_sem.at[2],
        ),
        pltpu.make_async_copy(table_in, table, local_sem.at[3]),
        pltpu.make_async_copy(inverse_in, inverse, local_sem.at[4]),
    ]
    for j in range(3):
        for h in range(2):
            piece = (j, h)
            left = pl.multiple_of(z * own + h * half, half)
            locals_.append(
                pltpu.make_async_copy(
                    wt.at[j, :, pl.ds(left, half)],
                    weight_rows(piece, pl.multiple_of(z * deep, deep), deep),
                    own_sem.at[number(piece)],
                )
            )
    for copy in locals_:
        copy.start()

    def relay_across(d):
        for k in range(2):
            for way in DIRECTIONS[: 1 if d == 0 else 2]:
                zb = z - way * d

                def step(k=k, zb=zb):
                    from_across(k, zb).wait_recv()
                    sibling(k, zb, True, False).start()

                pending.append((functools.partial(sibling, k, zb, True, False), valid(zb)))
                pl.when(valid(zb))(step)

    def relay_column(d):
        for k in range(2):
            for way in DIRECTIONS:
                zb = z - way * d
                on = jnp.logical_and(valid(zb), valid(z + way))

                def arrive(k=k, zb=zb, way=way):
                    column(k, zb, way, False).wait_recv()

                def after(k=k, zb=zb):
                    across(k, zb, False).start()
                    sibling(k, zb, False, False).start()

                pl.when(valid(zb))(arrive)
                launch(functools.partial(column, k, zb, way, False), on)
                pl.when(valid(zb))(after)
                pending.append((functools.partial(across, k, zb, False), valid(zb)))
                pending.append((functools.partial(sibling, k, zb, False, False), valid(zb)))

    def issue(make):
        for d in range(1, n):
            for way in DIRECTIONS:
                launch(functools.partial(make, z + way * d), valid(z + way * d))

    def each_source(step):
        for d in range(1, n):
            for way in DIRECTIONS:
                pl.when(valid(z - way * d))(functools.partial(step, z - way * d))

    def relay(take, give_on):
        def move(zb):
            take(zb).wait_recv()
            give_on(zb).start()

        each_source(move)
        for d in range(1, n):
            for way in DIRECTIONS:
                pending.append((functools.partial(give_on, z - way * d), valid(z - way * d)))

    def issue_weight(piece):
        issue(functools.partial(give_weight, piece))

    def relay_weight(piece):
        relay(functools.partial(take_weight, piece), functools.partial(pass_weight, piece))

    def finish_weight(piece):
        each_source(lambda zb: end_weight(piece, zb).wait_recv())

    def finish_tokens(d):
        for way in DIRECTIONS[: 1 if d == 0 else 2]:
            zb = z - way * d

            def finish(zb=zb):
                for k in range(2):
                    for xb in (x, 1 - x):
                        from_sibling(k, zb, xb).wait_recv()

            pl.when(valid(zb))(finish)

    def multiply_pair(h, zb):
        @pl.loop(0, 2)
        def _(k):
            top = pl.multiple_of(zb * rows, rows)
            to = pl.multiple_of(k * count + zb * rows, rows)
            p02[pl.ds(to, rows), :] = jnp.dot(
                full[k, pl.ds(top, rows), :], pairs[h], preferred_element_type=jnp.float32
            )

    def multiply_near(h, d):
        for way in DIRECTIONS[: 1 if d == 0 else 2]:
            pl.when(valid(z - way * d))(functools.partial(multiply_pair, h, z - way * d))

    def multiply_mid(h, zs, first):
        depth = pl.ds(pl.multiple_of(zs * deep, deep), deep)

        @pl.loop(0, 2 * n)
        def _(i):
            top = pl.multiple_of((i % n) * rows, rows)
            to = pl.ds(pl.multiple_of(i * rows, rows), rows)
            part = jnp.dot(
                full[i // n, pl.ds(top, rows), depth], mid[depth, pl.ds(h * half, half)],
                preferred_element_type=jnp.float32,
            )
            p1[to, :] = part if first else p1[to, :] + part

    line = lax.broadcasted_iota(jnp.int32, (count, half), 0)

    def forward(value, dst):
        high, low = split_value(value)
        xin[pl.ds(0, block), :] = high
        xin[pl.ds(block, block), :] = low
        xin[pl.ds(2 * block, block), :] = high

        @pl.loop(0, 2 * block // TILE)
        def _(m):
            at = pl.ds(pl.multiple_of(m * TILE, TILE), TILE)
            dst[at, :] = jnp.dot(table[at, :], xin[...], preferred_element_type=jnp.float32)

    def filter_spectra(h):
        lanes = pl.ds(h * half, half)
        for pair in range(blocks // 2):
            forward(
                jnp.concatenate(
                    [
                        ffull[pl.ds(2 * pair * block, block), lanes],
                        ffull[pl.ds((2 * pair + 1) * block, block), lanes],
                    ],
                    axis=1,
                ),
                plain.at[pair],
            )

        @pl.loop(0, 2 * block // STRIP)
        def _(m):
            at = pl.ds(pl.multiple_of(m * STRIP, STRIP), STRIP)
            row = lax.broadcasted_iota(jnp.int32, (STRIP, half), 0)
            sign = (1 - 2 * (row % 2)).astype(jnp.float32)
            before = None
            for b in range(blocks):
                left = (b % 2) * half
                here = plain[b // 2, at, left : left + half]
                kern[h, b, at, :] = here if before is None else here + sign * before
                before = here

    def filtered(ref, lanes, j, h, s):
        own_lanes = pl.ds(pl.multiple_of(z * own + h * half, half), half)
        value = ref[pl.ds(s * count, count), lanes]
        total = sw[0, pl.ds(j, 1), own_lanes] * value
        for o in range(1, taps):
            moved = jnp.where(line >= o, pltpu.roll(value, o, 0), 0.0)
            total = total + sw[o, pl.ds(j, 1), own_lanes] * moved
        return total

    def convolve(h):
        low_lanes, high_lanes = pl.ds(0, half), pl.ds(half, half)
        first_gate = filtered(p02, low_lanes, 0, h, 0)
        second_gate = filtered(p02, high_lanes, 2, h, 0)
        gates[:, :half] = first_gate * second_gate
        gates[:, half:] = filtered(p02, low_lanes, 0, h, 1) * second_gate + first_gate * filtered(
            p02, high_lanes, 2, h, 1
        )
        for b in range(blocks):
            forward(gates[pl.ds(b * block, block), :], spec.at[b])

        for b in range(blocks):

            @pl.loop(0, block // STRIP)
            def _(m):
                at = pl.ds(pl.multiple_of(m * STRIP, STRIP), STRIP)
                after = pl.ds(pl.multiple_of(block + m * STRIP, STRIP), STRIP)
                row = lax.broadcasted_iota(jnp.int32, (STRIP, 2 * half), 0) + m * STRIP
                first = row == 0
                weight = jnp.where(first, 0.5 / block, 1.0 / block)
                real, imag = 0.0, 0.0
                for a in range(b + 1):
                    kr, ki = kern[h, b - a, at, :], kern[h, b - a, after, :]
                    kr, ki = jnp.concatenate([kr, kr], axis=1), jnp.concatenate([ki, ki], axis=1)
                    vr, vi = spec[a, at, :], spec[a, after, :]
                    rr, ii = kr * vr, ki * vi
                    real = real + jnp.where(first, rr, rr - ii)
                    imag = imag + jnp.where(first, ii, kr * vi + ki * vr)
                for base, value in ((0, real), (block, imag)):
                    high, low = split_value(value * weight)
                    for third, part in enumerate((high, low, high)):
                        start = pl.multiple_of(third * 2 * block + base + m * STRIP, STRIP)
                        ycat[pl.ds(start, STRIP), :] = part

            @pl.loop(0, block // TILE)
            def _(m):
                at = pl.ds(pl.multiple_of(m * TILE, TILE), TILE)
                to = pl.ds(pl.multiple_of(b * block + m * TILE, TILE), TILE)
                conv[to, :] = jnp.dot(
                    inverse[at, :], ycat[...], preferred_element_type=jnp.float32
                )

    def give(h, o, target):
        top = pl.multiple_of(target * rows, rows)
        left = pl.multiple_of(z * own + h * half, half)
        return send(
            res.at[h, o, pl.ds(top, rows), :], outs[o].at[:, pl.ds(left, half)],
            send_sem.at[h, o, target], recv_sem.at[h, o, z], {"seq": target},
        )

    def take(h, o, source):
        top = pl.multiple_of(source * rows, rows)
        left = pl.multiple_of(source * own + h * half, half)
        return send(
            res.at[h, o, pl.ds(top, rows), :], outs[o].at[:, pl.ds(left, half)],
            send_sem.at[h, o, source], recv_sem.at[h, o, source], {"seq": source},
        )

    def keep(h, o):
        top = pl.multiple_of(z * rows, rows)
        left = pl.multiple_of(z * own + h * half, half)
        return pltpu.make_async_copy(
            res.at[h, o, pl.ds(top, rows), :], outs[o].at[:, pl.ds(left, half)], keep_sem.at[h, o]
        )

    def give_peak(h, target):
        left = pl.multiple_of(z * own + h * half, half)
        return send(
            top_of.at[h, target], peaks.at[:, pl.ds(left, half)],
            peak_send.at[h, target], peak_recv.at[h, z], {"seq": target},
        )

    def take_peak(h, source):
        left = pl.multiple_of(source * own + h * half, half)
        return send(
            top_of.at[h, source], peaks.at[:, pl.ds(left, half)],
            peak_send.at[h, source], peak_recv.at[h, source], {"seq": source},
        )

    def keep_peak(h):
        left = pl.multiple_of(z * own + h * half, half)
        return pltpu.make_async_copy(
            top_of.at[h, z], peaks.at[:, pl.ds(left, half)], peak_keep.at[h]
        )

    def answer(h):
        mids[:, :half] = filtered(p1, pl.ds(0, half), 1, h, 0)
        mids[:, half:] = filtered(p1, pl.ds(0, half), 1, h, 1)
        gain = skip[:, pl.ds(pl.multiple_of(z * own + h * half, half), half)]

        @pl.loop(0, n)
        def _(i):
            target = jnp.where(z < n // 2, n - 1 - i, i)

            def values(m, most):
                at = pl.ds(pl.multiple_of(target * rows + m * STRIP, STRIP), STRIP)
                combined = conv[at, :half] + gain * gates[at, :half]
                dcombined = conv[at, half:] + gain * gates[at, half:]
                middle = mids[at, :half]
                first = middle * combined
                second = mids[at, half:] * combined + middle * dcombined
                here = pl.ds(pl.multiple_of(m * STRIP, STRIP), STRIP)
                raw[0, here, :] = first
                raw[1, here, :] = second
                return tuple(
                    jnp.maximum(old, jnp.max(jnp.abs(new).reshape(STRIP // 8, 8, half), axis=0))
                    for old, new in zip(most, (first, second))
                )

            nothing = jnp.zeros((8, half), jnp.float32)
            most = lax.fori_loop(0, rows // STRIP, values, (nothing, nothing))
            for o in range(2):
                peak = jnp.maximum(jnp.max(most[o], axis=0, keepdims=True), TINY)
                top_of[h, target, pl.ds(8 * o, 8), :] = jnp.broadcast_to(peak, (8, half))
                scale = REACH / peak

                @pl.loop(0, rows // STRIP)
                def _(m):
                    here = pl.ds(pl.multiple_of(m * STRIP, STRIP), STRIP)
                    at = pl.ds(pl.multiple_of(target * rows + m * STRIP, STRIP), STRIP)
                    res[h, o, at, :] = encode(raw[o, here, :] * scale)

            @pl.when(target != z)
            def _():
                give_peak(h, target).start()
                for o in range(2):
                    give(h, o, target).start()

        keep_peak(h).start()
        for o in range(2):
            keep(h, o).start()

    pieces_a, pieces_b = ((0, 0), (2, 0)), ((0, 1), (2, 1))
    piece_c, piece_d = (1, 0), (1, 1)

    relay_column(1)
    issue(give_filter)
    for piece in pieces_a:
        issue_weight(piece)
    relay_across(0)
    relay_column(2)
    relay_across(1)
    issue_weight(piece_c)
    relay(take_filter, pass_filter)
    for piece in pieces_a:
        relay_weight(piece)
    for piece in pieces_b:
        issue_weight(piece)
    for copy in locals_:
        copy.wait()
    each_source(lambda zb: end_filter(zb).wait_recv())
    for h in range(2):
        filter_spectra(h)
    for piece in pieces_a:
        finish_weight(piece)
    for d in range(2):
        finish_tokens(d)
        multiply_near(0, d)
    relay_across(2)
    issue_weight(piece_d)
    for d in range(3, n):
        relay_column(d)
    relay_weight(piece_c)
    finish_tokens(2)
    multiply_near(0, 2)
    for d in range(3, n):
        relay_across(d)
        finish_tokens(d)
        multiply_near(0, d)
    convolve(0)
    for piece in pieces_b:
        relay_weight(piece)
    finish_weight(piece_c)

    @pl.loop(0, 2 * n)
    def _(i):
        top = pl.multiple_of((i % n) * rows, rows)
        to = pl.ds(pl.multiple_of(i * rows, rows), rows)
        p1[to, :] = jnp.dot(
            full[i // n, pl.ds(top, rows), :], mid[:, pl.ds(0, half)],
            preferred_element_type=jnp.float32,
        )

    answer(0)
    for piece in pieces_b:
        finish_weight(piece)

    @pl.loop(0, n)
    def _(zb):
        multiply_pair(1, zb)

    convolve(1)
    multiply_mid(1, z, True)

    def source(i):
        return jnp.where(z < n // 2, lax.rem(z + i, n), lax.rem(z + n - i, n))

    for i in range(1, n + 1):
        if i < n:
            take_weight(piece_d, source(i)).wait_recv()
            pass_weight(piece_d, source(i)).start()
            pending.append((functools.partial(pass_weight, piece_d, source(i)), None))
        if i > 1:
            end_weight(piece_d, source(i - 1)).wait_recv()
            multiply_mid(1, source(i - 1), False)
    answer(1)

    for make, condition in pending:
        if condition is None:
            make().wait_send()
        else:
            pl.when(condition)(lambda make=make: make().wait_send())
    for h in range(2):
        keep_peak(h).wait()
        for o in range(2):
            keep(h, o).wait()
        for d in range(1, n):
            for way in DIRECTIONS:
                there = z + way * d

                def finish(h=h, there=there):
                    take_peak(h, there).wait_recv()
                    give_peak(h, there).wait_send()
                    for o in range(2):
                        take(h, o, there).wait_recv()
                        give(h, o, there).wait_send()

                pl.when(valid(there))(finish)


def hyena(tokens, tangent, wt, long_filter, short_weight, skip_gain, block):
    n = lax.axis_size("seq")
    rows, wide = tokens.shape
    own = wt.shape[2] // n
    half, count = own // 2, rows * n
    blocks = count // block
    table = dft_table(block)
    vmem = pl.BlockSpec(memory_space=pltpu.VMEM)
    anywhere = pl.BlockSpec(memory_space=pl.ANY)
    sem = pltpu.SemaphoreType.DMA
    f32, bf16 = jnp.float32, jnp.bfloat16
    shape = jax.ShapeDtypeStruct((rows, own * n), bf16)
    first, second, peaks = pl.pallas_call(
        functools.partial(hyena_kernel, n, block),
        out_shape=(shape, shape, jax.ShapeDtypeStruct((16, own * n), f32)),
        in_specs=[anywhere] * 4 + [vmem] * 2 + [anywhere] * 2,
        out_specs=(anywhere,) * 3,
        scratch_shapes=[
            pltpu.VMEM((2, count, wide * 4), bf16),
            pltpu.VMEM((2, wt.shape[1] * n, own), bf16),
            pltpu.VMEM((wt.shape[1] * n, own), bf16),
            pltpu.VMEM((count, own), f32),
            pltpu.VMEM((2 * block, 3 * block), bf16),
            pltpu.VMEM((block, 6 * block), bf16),
            pltpu.VMEM((2 * count, own), f32),
            pltpu.VMEM((2 * count, half), f32),
            pltpu.VMEM((count, own), f32),
            pltpu.VMEM((count, own), f32),
            pltpu.VMEM((3 * block, own), bf16),
            pltpu.VMEM((blocks, 2 * block, own), f32),
            pltpu.VMEM((blocks // 2, 2 * block, own), f32),
            pltpu.VMEM((2, blocks, 2 * block, half), f32),
            pltpu.VMEM((6 * block, own), bf16),
            pltpu.VMEM((count, own), f32),
            pltpu.VMEM((2, rows, half), f32),
            pltpu.VMEM((2, 2, count, half), bf16),
            pltpu.VMEM((2, n, 16, half), f32),
            sem((5,)), sem((6,)),
            sem((2, n, 2)), sem((2, n)), sem((2, n)), sem((2, n)), sem((2, 2, n)), sem((2, 2, n)),
            sem((6, n)), sem((6, n)), sem((6, n)), sem((6, n)), sem((n,)), sem((n,)), sem((n,)), sem((n,)),
            sem((2, 2, n)), sem((2, 2, n)), sem((2, 2)),
            sem((2, n)), sem((2, n)), sem((2,)),
        ],
        compiler_params=pltpu.CompilerParams(
            collective_id=0, has_side_effects=True, vmem_limit_bytes=60 * 2**20
        ),
        name="hyena",
    )(
        tokens, tangent, wt, long_filter, short_weight, skip_gain.reshape(1, -1),
        jnp.asarray(split_table(table, 1)), jnp.asarray(split_table(table.T, 1)),
    )
    return decode(first, peaks[0:1]), decode(second, peaks[8:9])


def body(tokens, tangent, in_weight, short_weight, long_filter, skip_gain):
    devices = lax.axis_size("seq")
    shard = lax.axis_index("seq")
    own = in_weight.shape[2] // devices
    wt = in_weight.transpose(1, 0, 2)
    by_copies = own == 256 and devices == 4 and all(lax.axis_size(axis) == 2 for axis in ("grp", "chan", "sub"))
    block = min(512, long_filter.shape[0] * devices)
    if by_copies:
        return hyena(tokens, tangent, wt, long_filter, short_weight, skip_gain, block)

    both = jnp.stack([tokens, tangent])
    both = lax.all_gather(both, ("chan", "sub"), axis=2, tiled=True)
    both = lax.all_gather(both, "seq", axis=1, tiled=True)
    weight = lax.all_to_all(wt, "seq", split_axis=2, concat_axis=1, tiled=True)
    long_filter = lax.all_to_all(long_filter, "seq", split_axis=1, concat_axis=0, tiled=True)
    short_weight = lax.dynamic_slice_in_dim(short_weight, shard * own, own, axis=2)
    skip_gain = lax.dynamic_slice_in_dim(skip_gain, shard * own, own, axis=0)

    def project(values):
        return [jnp.dot(values, weight[j], preferred_element_type=jnp.float32) for j in range(3)]

    proj, dproj = project(both[0]), project(both[1])
    outs = operator(proj, dproj, short_weight, long_filter, skip_gain, block)
    return tuple(
        lax.all_to_all(value, "seq", split_axis=0, concat_axis=1, tiled=True) for value in outs
    )


def solution(mesh):
    placed = (
        P(("grp", "seq"), ("chan", "sub")),
        P(("grp", "seq"), ("chan", "sub")),
        P("seq", None, ("chan", "sub")),
        P(None, None, ("chan", "sub")),
        P("seq", ("chan", "sub")),
        P(("chan", "sub")),
    )
    return jax.shard_map(
        body,
        mesh=mesh,
        in_specs=placed,
        out_specs=(P(("grp", "seq"), ("chan", "sub")), P(("grp", "seq"), ("chan", "sub"))),
        check_vma=False,
    )
```

```python
import functools
import math

import jax
import jax.numpy as jnp
import numpy as np
from jax import lax
from jax.experimental import pallas as pl
from jax.experimental.pallas import tpu as pltpu
from jax.sharding import PartitionSpec as P

HIGH = lax.Precision.HIGH


def dft_table(block):
    size = 2 * block
    freqs = np.arange(block)[:, None]
    times = np.arange(block)[None, :]
    theta = (freqs * times % size) * (2.0 * math.pi / size)
    cosine = np.cos(theta)
    sine = -np.sin(theta)
    sine[0] = 1.0 - 2.0 * (np.arange(block) % 2)
    return np.concatenate([cosine, sine], axis=0).astype(np.float32)


def causal_convs(signals, long_filter, block):
    count = long_filter.shape[0]
    blocks = count // block
    table = jnp.asarray(dft_table(block))
    index = lax.broadcasted_iota(jnp.int32, (block, 1), 0)
    first = index == 0
    sign = (1 - 2 * (index % 2)).astype(jnp.float32)
    weight = jnp.where(first, 0.5 / block, 1.0 / block).astype(jnp.float32)

    def spectra(values):
        result = []
        for b in range(blocks):
            both = jnp.dot(table, values[b * block : (b + 1) * block], precision=HIGH)
            result.append((both[:block], both[block:]))
        return result

    plain = spectra(long_filter)
    kernels = [plain[0]]
    for b in range(1, blocks):
        kernels.append(tuple(here + sign * before for here, before in zip(plain[b], plain[b - 1])))
    outs = []
    for values in signals:
        moved = spectra(values)
        rows = []
        for b in range(blocks):
            real, imag = 0.0, 0.0
            for a in range(b + 1):
                kr, ki = kernels[b - a]
                vr, vi = moved[a]
                rr, ii = kr * vr, ki * vi
                real = real + jnp.where(first, rr, rr - ii)
                imag = imag + jnp.where(first, ii, kr * vi + ki * vr)
            packed = jnp.concatenate([real * weight, imag * weight], axis=0)
            rows.append(
                lax.dot_general(table, packed, (((0,), (0,)), ((), ())), precision=HIGH)
            )
        outs.append(jnp.concatenate(rows, axis=0))
    return outs


def short_filter(values, weights):
    count = values.shape[0]
    total = weights[0] * values
    for offset in range(1, weights.shape[0]):
        total = total + weights[offset] * jnp.pad(values, ((offset, 0), (0, 0)))[:count]
    return total


def operator(proj, dproj, short_weight, long_filter, skip_gain, block):
    mixed = [short_filter(proj[j], short_weight[:, j]) for j in range(3)]
    dmixed = [short_filter(dproj[j], short_weight[:, j]) for j in range(3)]
    gated_in = mixed[0] * mixed[2]
    dgated_in = dmixed[0] * mixed[2] + mixed[0] * dmixed[2]
    conv, dconv = causal_convs((gated_in, dgated_in), long_filter, block)
    combined = conv + skip_gain * gated_in
    dcombined = dconv + skip_gain * dgated_in
    return mixed[1] * combined, dmixed[1] * combined + mixed[1] * dcombined

MESH = pl.DeviceIdType.MESH
DIRECTIONS = (1, -1)


def split_table(table, axis):
    high = table.astype(jnp.bfloat16)
    low = (table - high.astype(np.float32)).astype(jnp.bfloat16)
    return np.concatenate([high, high, low], axis=axis)


def split_value(value):
    high = value.astype(jnp.bfloat16)
    return high, (value - high.astype(jnp.float32)).astype(jnp.bfloat16)


TILE = 256
STRIP = 64
POWER = 12
REACH = 1400.0
TINY = 1e-34


def encode(value):
    second = value * value
    fourth = second * second
    code = fourth * fourth * fourth
    return jnp.where(value < 0, -code, code).astype(jnp.bfloat16)


def decode(code, peak):
    value = code.astype(jnp.float32)
    size = jnp.exp2(jnp.log2(jnp.abs(value)) * (1.0 / POWER)) * (peak * (1.0 / REACH))
    return jnp.where(value < 0, -size, size)


def hyena_kernel(
    n, block, tok, tan, wt, filt, sw, skip, table_in, inverse_in, out0, out1, peaks,
    full, pairs, mid, ffull, table, inverse, p02, p1,
    gates, mids, xin, spec, plain, kern, ycat, conv, raw, res, top_of,
    local_sem, own_sem, col_send, col_recv, x_send, x_recv, c_send, c_recv,
    w_send, w_recv, y_send, y_recv, f_send, f_recv, fy_send, fy_recv,
    send_sem, recv_sem, keep_sem, peak_send, peak_recv, peak_keep,
):
    g, z = lax.axis_index("grp"), lax.axis_index("seq")
    x, c = lax.axis_index("chan"), lax.axis_index("sub")
    rows, wide = tok.shape
    count = rows * n
    deep, own = wt.shape[1], wt.shape[2] // n
    half, deep2, fhalf = own // 2, deep // 2, filt.shape[0] // 2
    blocks = count // block
    taps = sw.shape[0]
    sources = (tok, tan)
    outs = (out0, out1)
    pending = []

    def valid(place):
        return jnp.logical_and(place >= 0, place < n)

    def send(src, dst, send_sem, recv_sem, where):
        return pltpu.make_async_remote_copy(
            src_ref=src, dst_ref=dst, send_sem=send_sem, recv_sem=recv_sem,
            device_id=where, device_id_type=MESH,
        )

    def slot(k, zb, xb, cb):
        top = pl.multiple_of(zb * rows, rows)
        left = pl.multiple_of((xb * 2 + cb) * wide, wide)
        return full.at[k, pl.ds(top, rows), pl.ds(left, wide)]

    def column(k, zb, way, first):
        dst = slot(k, zb, x, c)
        src = sources[k] if first else dst
        lane = 0 if way > 0 else 1
        return send(src, dst, col_send.at[k, zb, lane], col_recv.at[k, zb], {"seq": z + way})

    def across(k, zb, first):
        dst = slot(k, zb, x, c)
        src = sources[k] if first else dst
        return send(src, dst, x_send.at[k, zb], x_recv.at[k, zb], {"chan": 1 - x})

    def sibling(k, zb, other, first):
        xb = 1 - x if other else x
        dst = slot(k, zb, xb, c)
        src = sources[k] if first else dst
        return send(src, dst, c_send.at[k, xb, zb], c_recv.at[k, xb, zb], {"sub": 1 - c})

    def from_sibling(k, zb, xb):
        dst = slot(k, zb, xb, 1 - c)
        return send(dst, dst, c_send.at[k, xb, zb], c_recv.at[k, xb, zb], {"sub": 1 - c})

    def from_across(k, zb):
        dst = slot(k, zb, 1 - x, c)
        return send(dst, dst, x_send.at[k, zb], x_recv.at[k, zb], {"chan": 1 - x})

    def weight_rows(piece, top, size):
        j, h = piece
        if j == 1:
            return mid.at[pl.ds(top, size), pl.ds(h * half, half)]
        return pairs.at[h, pl.ds(top, size), pl.ds((j // 2) * half, half)]

    def weight_part(piece, zb, gb):
        return weight_rows(piece, pl.multiple_of(zb * deep + gb * deep2, deep2), deep2)

    def filter_part(zb, gb):
        top = pl.multiple_of(zb * 2 * fhalf + gb * fhalf, fhalf)
        return ffull.at[pl.ds(top, fhalf), :]

    def number(piece):
        return piece[0] * 2 + piece[1]

    def give_weight(piece, target):
        left = pl.multiple_of(target * own + piece[1] * half, half)
        top = pl.multiple_of(g * deep2, deep2)
        src = wt.at[piece[0], pl.ds(top, deep2), pl.ds(left, half)]
        q = number(piece)
        return send(
            src, weight_part(piece, z, g), w_send.at[q, target], w_recv.at[q, z], {"seq": target}
        )

    def give_filter(target):
        left = pl.multiple_of(target * own, own)
        top = pl.multiple_of(g * fhalf, fhalf)
        src = filt.at[pl.ds(top, fhalf), pl.ds(left, own)]
        return send(src, filter_part(z, g), f_send.at[target], f_recv.at[z], {"seq": target})

    def take_weight(piece, zb):
        ref, q = weight_part(piece, zb, g), number(piece)
        return send(ref, ref, w_send.at[q, zb], w_recv.at[q, zb], {"seq": zb})

    def take_filter(zb):
        ref = filter_part(zb, g)
        return send(ref, ref, f_send.at[zb], f_recv.at[zb], {"seq": zb})

    def pass_weight(piece, zb):
        ref, q = weight_part(piece, zb, g), number(piece)
        return send(ref, ref, y_send.at[q, zb], y_recv.at[q, zb], {"grp": 1 - g})

    def pass_filter(zb):
        ref = filter_part(zb, g)
        return send(ref, ref, fy_send.at[zb], fy_recv.at[zb], {"grp": 1 - g})

    def end_weight(piece, zb):
        ref, q = weight_part(piece, zb, 1 - g), number(piece)
        return send(ref, ref, y_send.at[q, zb], y_recv.at[q, zb], {"grp": 1 - g})

    def end_filter(zb):
        ref = filter_part(zb, 1 - g)
        return send(ref, ref, fy_send.at[zb], fy_recv.at[zb], {"grp": 1 - g})

    barrier = pltpu.get_barrier_semaphore()
    for d in range(1, n):
        for way in DIRECTIONS:
            there = z + way * d

            @pl.when(valid(there))
            def _():
                pl.semaphore_signal(barrier, inc=1, device_id={"seq": there}, device_id_type=MESH)

    for where in ({"chan": 1 - x}, {"grp": 1 - g}, {"sub": 1 - c}):
        pl.semaphore_signal(barrier, inc=1, device_id=where, device_id_type=MESH)
    pl.semaphore_wait(barrier, n + 2)

    def launch(make, condition=None):
        pending.append((make, condition))
        if condition is None:
            make().start()
        else:
            pl.when(condition)(lambda: make().start())

    for k in range(2):
        for way in DIRECTIONS:
            launch(functools.partial(column, k, z, way, True), valid(z + way))
        launch(functools.partial(across, k, z, True))
        launch(functools.partial(sibling, k, z, False, True))
    mine = pl.ds(pl.multiple_of(z * own, own), own)
    locals_ = [
        pltpu.make_async_copy(tok, slot(0, z, x, c), local_sem.at[0]),
        pltpu.make_async_copy(tan, slot(1, z, x, c), local_sem.at[1]),
        pltpu.make_async_copy(
            filt.at[:, mine],
            ffull.at[pl.ds(pl.multiple_of(z * 2 * fhalf, 2 * fhalf), 2 * fhalf), :],
            local_sem.at[2],
        ),
        pltpu.make_async_copy(table_in, table, local_sem.at[3]),
        pltpu.make_async_copy(inverse_in, inverse, local_sem.at[4]),
    ]
    for j in range(3):
        for h in range(2):
            piece = (j, h)
            left = pl.multiple_of(z * own + h * half, half)
            locals_.append(
                pltpu.make_async_copy(
                    wt.at[j, :, pl.ds(left, half)],
                    weight_rows(piece, pl.multiple_of(z * deep, deep), deep),
                    own_sem.at[number(piece)],
                )
            )
    for copy in locals_:
        copy.start()

    def relay_across(d):
        for k in range(2):
            for way in DIRECTIONS[: 1 if d == 0 else 2]:
                zb = z - way * d

                def step(k=k, zb=zb):
                    from_across(k, zb).wait_recv()
                    sibling(k, zb, True, False).start()

                pending.append((functools.partial(sibling, k, zb, True, False), valid(zb)))
                pl.when(valid(zb))(step)

    def relay_column(d):
        for k in range(2):
            for way in DIRECTIONS:
                zb = z - way * d
                on = jnp.logical_and(valid(zb), valid(z + way))

                def arrive(k=k, zb=zb, way=way):
                    column(k, zb, way, False).wait_recv()

                def after(k=k, zb=zb):
                    across(k, zb, False).start()
                    sibling(k, zb, False, False).start()

                pl.when(valid(zb))(arrive)
                launch(functools.partial(column, k, zb, way, False), on)
                pl.when(valid(zb))(after)
                pending.append((functools.partial(across, k, zb, False), valid(zb)))
                pending.append((functools.partial(sibling, k, zb, False, False), valid(zb)))

    def issue(make):
        for d in range(1, n):
            for way in DIRECTIONS:
                launch(functools.partial(make, z + way * d), valid(z + way * d))

    def each_source(step):
        for d in range(1, n):
            for way in DIRECTIONS:
                pl.when(valid(z - way * d))(functools.partial(step, z - way * d))

    def relay(take, give_on):
        def move(zb):
            take(zb).wait_recv()
            give_on(zb).start()

        each_source(move)
        for d in range(1, n):
            for way in DIRECTIONS:
                pending.append((functools.partial(give_on, z - way * d), valid(z - way * d)))

    def issue_weight(piece):
        issue(functools.partial(give_weight, piece))

    def relay_weight(piece):
        relay(functools.partial(take_weight, piece), functools.partial(pass_weight, piece))

    def finish_weight(piece):
        each_source(lambda zb: end_weight(piece, zb).wait_recv())

    def finish_tokens(d):
        for way in DIRECTIONS[: 1 if d == 0 else 2]:
            zb = z - way * d

            def finish(zb=zb):
                for k in range(2):
                    for xb in (x, 1 - x):
                        from_sibling(k, zb, xb).wait_recv()

            pl.when(valid(zb))(finish)

    def multiply_pair(h, zb):
        @pl.loop(0, 2)
        def _(k):
            top = pl.multiple_of(zb * rows, rows)
            to = pl.multiple_of(k * count + zb * rows, rows)
            p02[pl.ds(to, rows), :] = jnp.dot(
                full[k, pl.ds(top, rows), :], pairs[h], preferred_element_type=jnp.float32
            )

    def near(multiply, h, d):
        for way in DIRECTIONS[: 1 if d == 0 else 2]:
            pl.when(valid(z - way * d))(functools.partial(multiply, h, z - way * d))

    def multiply_rows(h, zb):
        @pl.loop(0, 2)
        def _(k):
            top = pl.multiple_of(zb * rows, rows)
            to = pl.multiple_of(k * count + zb * rows, rows)
            p1[pl.ds(to, rows), :] = jnp.dot(
                full[k, pl.ds(top, rows), :], mid[:, pl.ds(h * half, half)],
                preferred_element_type=jnp.float32,
            )

    def multiply_mid(h, zs, first):
        depth = pl.ds(pl.multiple_of(zs * deep, deep), deep)

        @pl.loop(0, 2 * n)
        def _(i):
            top = pl.multiple_of((i % n) * rows, rows)
            to = pl.ds(pl.multiple_of(i * rows, rows), rows)
            part = jnp.dot(
                full[i // n, pl.ds(top, rows), depth], mid[depth, pl.ds(h * half, half)],
                preferred_element_type=jnp.float32,
            )
            p1[to, :] = part if first else p1[to, :] + part

    line = lax.broadcasted_iota(jnp.int32, (count, half), 0)

    def forward(value, dst):
        high, low = split_value(value)
        xin[pl.ds(0, block), :] = high
        xin[pl.ds(block, block), :] = low
        xin[pl.ds(2 * block, block), :] = high

        @pl.loop(0, 2 * block // TILE)
        def _(m):
            at = pl.ds(pl.multiple_of(m * TILE, TILE), TILE)
            dst[at, :] = jnp.dot(table[at, :], xin[...], preferred_element_type=jnp.float32)

    def filter_spectra(h):
        lanes = pl.ds(h * half, half)
        for pair in range(blocks // 2):
            forward(
                jnp.concatenate(
                    [
                        ffull[pl.ds(2 * pair * block, block), lanes],
                        ffull[pl.ds((2 * pair + 1) * block, block), lanes],
                    ],
                    axis=1,
                ),
                plain.at[pair],
            )

        @pl.loop(0, 2 * block // STRIP)
        def _(m):
            at = pl.ds(pl.multiple_of(m * STRIP, STRIP), STRIP)
            row = lax.broadcasted_iota(jnp.int32, (STRIP, half), 0)
            sign = (1 - 2 * (row % 2)).astype(jnp.float32)
            before = None
            for b in range(blocks):
                left = (b % 2) * half
                here = plain[b // 2, at, left : left + half]
                kern[h, b, at, :] = here if before is None else here + sign * before
                before = here

    def filtered(ref, lanes, j, h, s):
        own_lanes = pl.ds(pl.multiple_of(z * own + h * half, half), half)
        value = ref[pl.ds(s * count, count), lanes]
        total = sw[0, pl.ds(j, 1), own_lanes] * value
        for o in range(1, taps):
            moved = jnp.where(line >= o, pltpu.roll(value, o, 0), 0.0)
            total = total + sw[o, pl.ds(j, 1), own_lanes] * moved
        return total

    def transform(h):
        low_lanes, high_lanes = pl.ds(0, half), pl.ds(half, half)
        first_gate = filtered(p02, low_lanes, 0, h, 0)
        second_gate = filtered(p02, high_lanes, 2, h, 0)
        gates[:, :half] = first_gate * second_gate
        gates[:, half:] = filtered(p02, low_lanes, 0, h, 1) * second_gate + first_gate * filtered(
            p02, high_lanes, 2, h, 1
        )
        for b in range(blocks):
            forward(gates[pl.ds(b * block, block), :], spec.at[b])

    def convolve(h):
        for b in range(blocks):

            @pl.loop(0, block // STRIP)
            def _(m):
                at = pl.ds(pl.multiple_of(m * STRIP, STRIP), STRIP)
                after = pl.ds(pl.multiple_of(block + m * STRIP, STRIP), STRIP)
                row = lax.broadcasted_iota(jnp.int32, (STRIP, 2 * half), 0) + m * STRIP
                first = row == 0
                weight = jnp.where(first, 0.5 / block, 1.0 / block)
                real, imag = 0.0, 0.0
                for a in range(b + 1):
                    kr, ki = kern[h, b - a, at, :], kern[h, b - a, after, :]
                    kr, ki = jnp.concatenate([kr, kr], axis=1), jnp.concatenate([ki, ki], axis=1)
                    vr, vi = spec[a, at, :], spec[a, after, :]
                    rr, ii = kr * vr, ki * vi
                    real = real + jnp.where(first, rr, rr - ii)
                    imag = imag + jnp.where(first, ii, kr * vi + ki * vr)
                for base, value in ((0, real), (block, imag)):
                    high, low = split_value(value * weight)
                    for third, part in enumerate((high, low, high)):
                        start = pl.multiple_of(third * 2 * block + base + m * STRIP, STRIP)
                        ycat[pl.ds(start, STRIP), :] = part

            @pl.loop(0, block // TILE)
            def _(m):
                at = pl.ds(pl.multiple_of(m * TILE, TILE), TILE)
                to = pl.ds(pl.multiple_of(b * block + m * TILE, TILE), TILE)
                conv[to, :] = jnp.dot(
                    inverse[at, :], ycat[...], preferred_element_type=jnp.float32
                )

    def give(h, o, target):
        top = pl.multiple_of(target * rows, rows)
        left = pl.multiple_of(z * own + h * half, half)
        return send(
            res.at[h, o, pl.ds(top, rows), :], outs[o].at[:, pl.ds(left, half)],
            send_sem.at[h, o, target], recv_sem.at[h, o, z], {"seq": target},
        )

    def take(h, o, source):
        top = pl.multiple_of(source * rows, rows)
        left = pl.multiple_of(source * own + h * half, half)
        return send(
            res.at[h, o, pl.ds(top, rows), :], outs[o].at[:, pl.ds(left, half)],
            send_sem.at[h, o, source], recv_sem.at[h, o, source], {"seq": source},
        )

    def keep(h, o):
        top = pl.multiple_of(z * rows, rows)
        left = pl.multiple_of(z * own + h * half, half)
        return pltpu.make_async_copy(
            res.at[h, o, pl.ds(top, rows), :], outs[o].at[:, pl.ds(left, half)], keep_sem.at[h, o]
        )

    def give_peak(h, target):
        left = pl.multiple_of(z * own + h * half, half)
        return send(
            top_of.at[h, target], peaks.at[:, pl.ds(left, half)],
            peak_send.at[h, target], peak_recv.at[h, z], {"seq": target},
        )

    def take_peak(h, source):
        left = pl.multiple_of(source * own + h * half, half)
        return send(
            top_of.at[h, source], peaks.at[:, pl.ds(left, half)],
            peak_send.at[h, source], peak_recv.at[h, source], {"seq": source},
        )

    def keep_peak(h):
        left = pl.multiple_of(z * own + h * half, half)
        return pltpu.make_async_copy(
            top_of.at[h, z], peaks.at[:, pl.ds(left, half)], peak_keep.at[h]
        )

    def answer(h):
        mids[:, :half] = filtered(p1, pl.ds(0, half), 1, h, 0)
        mids[:, half:] = filtered(p1, pl.ds(0, half), 1, h, 1)
        gain = skip[:, pl.ds(pl.multiple_of(z * own + h * half, half), half)]

        @pl.loop(0, n)
        def _(i):
            target = jnp.where(z < n // 2, n - 1 - i, i)

            def values(m, most):
                at = pl.ds(pl.multiple_of(target * rows + m * STRIP, STRIP), STRIP)
                combined = conv[at, :half] + gain * gates[at, :half]
                dcombined = conv[at, half:] + gain * gates[at, half:]
                middle = mids[at, :half]
                first = middle * combined
                second = mids[at, half:] * combined + middle * dcombined
                here = pl.ds(pl.multiple_of(m * STRIP, STRIP), STRIP)
                raw[0, here, :] = first
                raw[1, here, :] = second
                return tuple(
                    jnp.maximum(old, jnp.max(jnp.abs(new).reshape(STRIP // 8, 8, half), axis=0))
                    for old, new in zip(most, (first, second))
                )

            nothing = jnp.zeros((8, half), jnp.float32)
            most = lax.fori_loop(0, rows // STRIP, values, (nothing, nothing))
            for o in range(2):
                peak = jnp.maximum(jnp.max(most[o], axis=0, keepdims=True), TINY)
                top_of[h, target, pl.ds(8 * o, 8), :] = jnp.broadcast_to(peak, (8, half))
                scale = REACH / peak

                @pl.loop(0, rows // STRIP)
                def _(m):
                    here = pl.ds(pl.multiple_of(m * STRIP, STRIP), STRIP)
                    at = pl.ds(pl.multiple_of(target * rows + m * STRIP, STRIP), STRIP)
                    res[h, o, at, :] = encode(raw[o, here, :] * scale)

            @pl.when(target != z)
            def _():
                give_peak(h, target).start()
                for o in range(2):
                    give(h, o, target).start()

        keep_peak(h).start()
        for o in range(2):
            keep(h, o).start()

    def issue_filter():
        issue(give_filter)

    def relay_filter():
        relay(take_filter, pass_filter)

    first_pair, second_pair = ((0, 0), (2, 0)), ((0, 1), (2, 1))
    first_mid, second_mid = (1, 0), (1, 1)

    relay_column(1)
    issue_filter()
    for piece in first_pair:
        issue_weight(piece)
    relay_across(0)
    relay_column(2)
    relay_across(1)
    relay_filter()
    issue_weight(first_mid)
    for piece, following in zip(first_pair, second_pair):
        relay_weight(piece)
        issue_weight(following)
    for copy in locals_:
        copy.wait()
    each_source(lambda zb: end_filter(zb).wait_recv())
    for h in range(2):
        filter_spectra(h)
    for piece in first_pair:
        finish_weight(piece)
    for d in range(2):
        finish_tokens(d)
        near(multiply_pair, 0, d)
    for d in range(3, n):
        relay_column(d)
    relay_across(2)
    issue_weight(second_mid)
    relay_weight(first_mid)
    finish_tokens(2)
    near(multiply_pair, 0, 2)
    relay_weight(second_pair[0])
    finish_weight(first_mid)
    for d in range(3):
        near(multiply_rows, 0, d)
    for d in range(3, n):
        relay_across(d)
        finish_tokens(d)
        near(multiply_pair, 0, d)
    transform(0)
    relay_weight(second_pair[1])
    convolve(0)
    for d in range(3, n):
        near(multiply_rows, 0, d)
    answer(0)
    for piece in second_pair:
        finish_weight(piece)

    @pl.loop(0, n)
    def _(zb):
        multiply_pair(1, zb)

    transform(1)
    convolve(1)
    multiply_mid(1, z, True)

    def source(i):
        return jnp.where(z < n // 2, lax.rem(z + i, n), lax.rem(z + n - i, n))

    for i in range(1, n + 1):
        if i < n:
            take_weight(second_mid, source(i)).wait_recv()
            pass_weight(second_mid, source(i)).start()
            pending.append((functools.partial(pass_weight, second_mid, source(i)), None))
        if i > 1:
            end_weight(second_mid, source(i - 1)).wait_recv()
            multiply_mid(1, source(i - 1), False)
    answer(1)

    for make, condition in pending:
        if condition is None:
            make().wait_send()
        else:
            pl.when(condition)(lambda make=make: make().wait_send())
    for h in range(2):
        keep_peak(h).wait()
        for o in range(2):
            keep(h, o).wait()
        for d in range(1, n):
            for way in DIRECTIONS:
                there = z + way * d

                def finish(h=h, there=there):
                    take_peak(h, there).wait_recv()
                    give_peak(h, there).wait_send()
                    for o in range(2):
                        take(h, o, there).wait_recv()
                        give(h, o, there).wait_send()

                pl.when(valid(there))(finish)


def hyena(tokens, tangent, wt, long_filter, short_weight, skip_gain, block):
    n = lax.axis_size("seq")
    rows, wide = tokens.shape
    own = wt.shape[2] // n
    half, count = own // 2, rows * n
    blocks = count // block
    table = dft_table(block)
    vmem = pl.BlockSpec(memory_space=pltpu.VMEM)
    anywhere = pl.BlockSpec(memory_space=pl.ANY)
    sem = pltpu.SemaphoreType.DMA
    f32, bf16 = jnp.float32, jnp.bfloat16
    shape = jax.ShapeDtypeStruct((rows, own * n), bf16)
    first, second, peaks = pl.pallas_call(
        functools.partial(hyena_kernel, n, block),
        out_shape=(shape, shape, jax.ShapeDtypeStruct((16, own * n), f32)),
        in_specs=[anywhere] * 4 + [vmem] * 2 + [anywhere] * 2,
        out_specs=(anywhere,) * 3,
        scratch_shapes=[
            pltpu.VMEM((2, count, wide * 4), bf16),
            pltpu.VMEM((2, wt.shape[1] * n, own), bf16),
            pltpu.VMEM((wt.shape[1] * n, own), bf16),
            pltpu.VMEM((count, own), f32),
            pltpu.VMEM((2 * block, 3 * block), bf16),
            pltpu.VMEM((block, 6 * block), bf16),
            pltpu.VMEM((2 * count, own), f32),
            pltpu.VMEM((2 * count, half), f32),
            pltpu.VMEM((count, own), f32),
            pltpu.VMEM((count, own), f32),
            pltpu.VMEM((3 * block, own), bf16),
            pltpu.VMEM((blocks, 2 * block, own), f32),
            pltpu.VMEM((blocks // 2, 2 * block, own), f32),
            pltpu.VMEM((2, blocks, 2 * block, half), f32),
            pltpu.VMEM((6 * block, own), bf16),
            pltpu.VMEM((count, own), f32),
            pltpu.VMEM((2, rows, half), f32),
            pltpu.VMEM((2, 2, count, half), bf16),
            pltpu.VMEM((2, n, 16, half), f32),
            sem((5,)), sem((6,)),
            sem((2, n, 2)), sem((2, n)), sem((2, n)), sem((2, n)), sem((2, 2, n)), sem((2, 2, n)),
            sem((6, n)), sem((6, n)), sem((6, n)), sem((6, n)), sem((n,)), sem((n,)), sem((n,)), sem((n,)),
            sem((2, 2, n)), sem((2, 2, n)), sem((2, 2)),
            sem((2, n)), sem((2, n)), sem((2,)),
        ],
        compiler_params=pltpu.CompilerParams(
            collective_id=0, has_side_effects=True, vmem_limit_bytes=60 * 2**20
        ),
        name="hyena",
    )(
        tokens, tangent, wt, long_filter, short_weight, skip_gain.reshape(1, -1),
        jnp.asarray(split_table(table, 1)), jnp.asarray(split_table(table.T, 1)),
    )
    return decode(first, peaks[0:1]), decode(second, peaks[8:9])


def body(tokens, tangent, in_weight, short_weight, long_filter, skip_gain):
    devices = lax.axis_size("seq")
    shard = lax.axis_index("seq")
    own = in_weight.shape[2] // devices
    wt = in_weight.transpose(1, 0, 2)
    by_copies = own == 256 and devices == 4 and all(lax.axis_size(axis) == 2 for axis in ("grp", "chan", "sub"))
    block = min(512, long_filter.shape[0] * devices)
    if by_copies:
        return hyena(tokens, tangent, wt, long_filter, short_weight, skip_gain, block)

    both = jnp.stack([tokens, tangent])
    both = lax.all_gather(both, ("chan", "sub"), axis=2, tiled=True)
    both = lax.all_gather(both, "seq", axis=1, tiled=True)
    weight = lax.all_to_all(wt, "seq", split_axis=2, concat_axis=1, tiled=True)
    long_filter = lax.all_to_all(long_filter, "seq", split_axis=1, concat_axis=0, tiled=True)
    short_weight = lax.dynamic_slice_in_dim(short_weight, shard * own, own, axis=2)
    skip_gain = lax.dynamic_slice_in_dim(skip_gain, shard * own, own, axis=0)

    def project(values):
        return [jnp.dot(values, weight[j], preferred_element_type=jnp.float32) for j in range(3)]

    proj, dproj = project(both[0]), project(both[1])
    outs = operator(proj, dproj, short_weight, long_filter, skip_gain, block)
    return tuple(
        lax.all_to_all(value, "seq", split_axis=0, concat_axis=1, tiled=True) for value in outs
    )


def solution(mesh):
    placed = (
        P(("grp", "seq"), ("chan", "sub")),
        P(("grp", "seq"), ("chan", "sub")),
        P("seq", None, ("chan", "sub")),
        P(None, None, ("chan", "sub")),
        P("seq", ("chan", "sub")),
        P(("chan", "sub")),
    )
    return jax.shard_map(
        body,
        mesh=mesh,
        in_specs=placed,
        out_specs=(P(("grp", "seq"), ("chan", "sub")), P(("grp", "seq"), ("chan", "sub"))),
        check_vma=False,
    )
```

```python
import functools
import math

import jax
import jax.numpy as jnp
import numpy as np
from jax import lax
from jax.experimental import pallas as pl
from jax.experimental.pallas import tpu as pltpu
from jax.sharding import PartitionSpec as P

HIGH = lax.Precision.HIGH


def dft_table(block):
    size = 2 * block
    freqs = np.arange(block)[:, None]
    times = np.arange(block)[None, :]
    theta = (freqs * times % size) * (2.0 * math.pi / size)
    cosine = np.cos(theta)
    sine = -np.sin(theta)
    sine[0] = 1.0 - 2.0 * (np.arange(block) % 2)
    return np.concatenate([cosine, sine], axis=0).astype(np.float32)


def causal_convs(signals, long_filter, block):
    count = long_filter.shape[0]
    blocks = count // block
    table = jnp.asarray(dft_table(block))
    index = lax.broadcasted_iota(jnp.int32, (block, 1), 0)
    first = index == 0
    sign = (1 - 2 * (index % 2)).astype(jnp.float32)
    weight = jnp.where(first, 0.5 / block, 1.0 / block).astype(jnp.float32)

    def spectra(values):
        result = []
        for b in range(blocks):
            both = jnp.dot(table, values[b * block : (b + 1) * block], precision=HIGH)
            result.append((both[:block], both[block:]))
        return result

    plain = spectra(long_filter)
    kernels = [plain[0]]
    for b in range(1, blocks):
        kernels.append(tuple(here + sign * before for here, before in zip(plain[b], plain[b - 1])))
    outs = []
    for values in signals:
        moved = spectra(values)
        rows = []
        for b in range(blocks):
            real, imag = 0.0, 0.0
            for a in range(b + 1):
                kr, ki = kernels[b - a]
                vr, vi = moved[a]
                rr, ii = kr * vr, ki * vi
                real = real + jnp.where(first, rr, rr - ii)
                imag = imag + jnp.where(first, ii, kr * vi + ki * vr)
            packed = jnp.concatenate([real * weight, imag * weight], axis=0)
            rows.append(
                lax.dot_general(table, packed, (((0,), (0,)), ((), ())), precision=HIGH)
            )
        outs.append(jnp.concatenate(rows, axis=0))
    return outs


def short_filter(values, weights):
    count = values.shape[0]
    total = weights[0] * values
    for offset in range(1, weights.shape[0]):
        total = total + weights[offset] * jnp.pad(values, ((offset, 0), (0, 0)))[:count]
    return total


def operator(proj, dproj, short_weight, long_filter, skip_gain, block):
    mixed = [short_filter(proj[j], short_weight[:, j]) for j in range(3)]
    dmixed = [short_filter(dproj[j], short_weight[:, j]) for j in range(3)]
    gated_in = mixed[0] * mixed[2]
    dgated_in = dmixed[0] * mixed[2] + mixed[0] * dmixed[2]
    conv, dconv = causal_convs((gated_in, dgated_in), long_filter, block)
    combined = conv + skip_gain * gated_in
    dcombined = dconv + skip_gain * dgated_in
    return mixed[1] * combined, dmixed[1] * combined + mixed[1] * dcombined

MESH = pl.DeviceIdType.MESH
DIRECTIONS = (1, -1)


def split_table(table, axis):
    high = table.astype(jnp.bfloat16)
    low = (table - high.astype(np.float32)).astype(jnp.bfloat16)
    return np.concatenate([high, high, low], axis=axis)


def split_value(value):
    high = value.astype(jnp.bfloat16)
    return high, (value - high.astype(jnp.float32)).astype(jnp.bfloat16)


TILE = 256
STRIP = 64
POWER = 12
REACH = 1400.0
TINY = 1e-34


def encode(value):
    second = value * value
    fourth = second * second
    code = fourth * fourth * fourth
    return jnp.where(value < 0, -code, code).astype(jnp.bfloat16)


def decode(code, unit):
    value = code.astype(jnp.float32).reshape(-1, *unit.shape)
    size = jnp.exp2(jnp.log2(jnp.abs(value)) * (1.0 / POWER)) * unit
    return jnp.where(value < 0, -size, size).reshape(code.shape)


def hyena_kernel(
    n, block, tok, tan, wt, filt, sw, skip, table_in, inverse_in, out0, out1, unit0, unit1,
    full, pairs, mid, ffull, table, inverse, p02, p1,
    gates, mids, xin, spec, plain, kern, ycat, conv, raw, res, top_of,
    local_sem, own_sem, col_send, col_recv, x_send, x_recv, c_send, c_recv,
    w_send, w_recv, y_send, y_recv, f_send, f_recv, fy_send, fy_recv,
    send_sem, recv_sem, keep_sem, unit_send, unit_recv, unit_keep,
):
    g, z = lax.axis_index("grp"), lax.axis_index("seq")
    x, c = lax.axis_index("chan"), lax.axis_index("sub")
    rows, wide = tok.shape
    count = rows * n
    deep, own = wt.shape[1], wt.shape[2] // n
    half, deep2, fhalf = own // 2, deep // 2, filt.shape[0] // 2
    blocks = count // block
    taps = sw.shape[0]
    sources = (tok, tan)
    outs = (out0, out1)
    units = (unit0, unit1)
    pending = []

    def valid(place):
        return jnp.logical_and(place >= 0, place < n)

    def send(src, dst, send_sem, recv_sem, where):
        return pltpu.make_async_remote_copy(
            src_ref=src, dst_ref=dst, send_sem=send_sem, recv_sem=recv_sem,
            device_id=where, device_id_type=MESH,
        )

    def slot(k, zb, xb, cb):
        top = pl.multiple_of(zb * rows, rows)
        left = pl.multiple_of((xb * 2 + cb) * wide, wide)
        return full.at[k, pl.ds(top, rows), pl.ds(left, wide)]

    def column(k, zb, way, first):
        dst = slot(k, zb, x, c)
        src = sources[k] if first else dst
        lane = 0 if way > 0 else 1
        return send(src, dst, col_send.at[k, zb, lane], col_recv.at[k, zb], {"seq": z + way})

    def across(k, zb, first):
        dst = slot(k, zb, x, c)
        src = sources[k] if first else dst
        return send(src, dst, x_send.at[k, zb], x_recv.at[k, zb], {"chan": 1 - x})

    def sibling(k, zb, other, first):
        xb = 1 - x if other else x
        dst = slot(k, zb, xb, c)
        src = sources[k] if first else dst
        return send(src, dst, c_send.at[k, xb, zb], c_recv.at[k, xb, zb], {"sub": 1 - c})

    def from_sibling(k, zb, xb):
        dst = slot(k, zb, xb, 1 - c)
        return send(dst, dst, c_send.at[k, xb, zb], c_recv.at[k, xb, zb], {"sub": 1 - c})

    def from_across(k, zb):
        dst = slot(k, zb, 1 - x, c)
        return send(dst, dst, x_send.at[k, zb], x_recv.at[k, zb], {"chan": 1 - x})

    def weight_rows(piece, top, size):
        j, h = piece
        if j == 1:
            return mid.at[pl.ds(top, size), pl.ds(h * half, half)]
        return pairs.at[h, pl.ds(top, size), pl.ds((j // 2) * half, half)]

    def weight_part(piece, zb, gb):
        return weight_rows(piece, pl.multiple_of(zb * deep + gb * deep2, deep2), deep2)

    def filter_part(zb, gb):
        top = pl.multiple_of(zb * 2 * fhalf + gb * fhalf, fhalf)
        return ffull.at[pl.ds(top, fhalf), :]

    def number(piece):
        return piece[0] * 2 + piece[1]

    def give_weight(piece, target):
        left = pl.multiple_of(target * own + piece[1] * half, half)
        top = pl.multiple_of(g * deep2, deep2)
        src = wt.at[piece[0], pl.ds(top, deep2), pl.ds(left, half)]
        q = number(piece)
        return send(
            src, weight_part(piece, z, g), w_send.at[q, target], w_recv.at[q, z], {"seq": target}
        )

    def give_filter(target):
        left = pl.multiple_of(target * own, own)
        top = pl.multiple_of(g * fhalf, fhalf)
        src = filt.at[pl.ds(top, fhalf), pl.ds(left, own)]
        return send(src, filter_part(z, g), f_send.at[target], f_recv.at[z], {"seq": target})

    def take_weight(piece, zb):
        ref, q = weight_part(piece, zb, g), number(piece)
        return send(ref, ref, w_send.at[q, zb], w_recv.at[q, zb], {"seq": zb})

    def take_filter(zb):
        ref = filter_part(zb, g)
        return send(ref, ref, f_send.at[zb], f_recv.at[zb], {"seq": zb})

    def pass_weight(piece, zb):
        ref, q = weight_part(piece, zb, g), number(piece)
        return send(ref, ref, y_send.at[q, zb], y_recv.at[q, zb], {"grp": 1 - g})

    def pass_filter(zb):
        ref = filter_part(zb, g)
        return send(ref, ref, fy_send.at[zb], fy_recv.at[zb], {"grp": 1 - g})

    def end_weight(piece, zb):
        ref, q = weight_part(piece, zb, 1 - g), number(piece)
        return send(ref, ref, y_send.at[q, zb], y_recv.at[q, zb], {"grp": 1 - g})

    def end_filter(zb):
        ref = filter_part(zb, 1 - g)
        return send(ref, ref, fy_send.at[zb], fy_recv.at[zb], {"grp": 1 - g})

    barrier = pltpu.get_barrier_semaphore()
    for d in range(1, n):
        for way in DIRECTIONS:
            there = z + way * d

            @pl.when(valid(there))
            def _():
                pl.semaphore_signal(barrier, inc=1, device_id={"seq": there}, device_id_type=MESH)

    for where in ({"chan": 1 - x}, {"grp": 1 - g}, {"sub": 1 - c}):
        pl.semaphore_signal(barrier, inc=1, device_id=where, device_id_type=MESH)
    pl.semaphore_wait(barrier, n + 2)

    def launch(make, condition=None):
        pending.append((make, condition))
        if condition is None:
            make().start()
        else:
            pl.when(condition)(lambda: make().start())

    for k in range(2):
        for way in DIRECTIONS:
            launch(functools.partial(column, k, z, way, True), valid(z + way))
        launch(functools.partial(across, k, z, True))
        launch(functools.partial(sibling, k, z, False, True))
    mine = pl.ds(pl.multiple_of(z * own, own), own)
    locals_ = [
        pltpu.make_async_copy(tok, slot(0, z, x, c), local_sem.at[0]),
        pltpu.make_async_copy(tan, slot(1, z, x, c), local_sem.at[1]),
        pltpu.make_async_copy(
            filt.at[:, mine],
            ffull.at[pl.ds(pl.multiple_of(z * 2 * fhalf, 2 * fhalf), 2 * fhalf), :],
            local_sem.at[2],
        ),
        pltpu.make_async_copy(table_in, table, local_sem.at[3]),
        pltpu.make_async_copy(inverse_in, inverse, local_sem.at[4]),
    ]
    for j in range(3):
        for h in range(2):
            piece = (j, h)
            left = pl.multiple_of(z * own + h * half, half)
            locals_.append(
                pltpu.make_async_copy(
                    wt.at[j, :, pl.ds(left, half)],
                    weight_rows(piece, pl.multiple_of(z * deep, deep), deep),
                    own_sem.at[number(piece)],
                )
            )
    for copy in locals_:
        copy.start()

    def relay_across(d):
        for k in range(2):
            for way in DIRECTIONS[: 1 if d == 0 else 2]:
                zb = z - way * d

                def step(k=k, zb=zb):
                    from_across(k, zb).wait_recv()
                    sibling(k, zb, True, False).start()

                pending.append((functools.partial(sibling, k, zb, True, False), valid(zb)))
                pl.when(valid(zb))(step)

    def relay_column(d):
        for k in range(2):
            for way in DIRECTIONS:
                zb = z - way * d
                on = jnp.logical_and(valid(zb), valid(z + way))

                def arrive(k=k, zb=zb, way=way):
                    column(k, zb, way, False).wait_recv()

                def after(k=k, zb=zb):
                    across(k, zb, False).start()
                    sibling(k, zb, False, False).start()

                pl.when(valid(zb))(arrive)
                launch(functools.partial(column, k, zb, way, False), on)
                pl.when(valid(zb))(after)
                pending.append((functools.partial(across, k, zb, False), valid(zb)))
                pending.append((functools.partial(sibling, k, zb, False, False), valid(zb)))

    def issue(make):
        for d in range(1, n):
            for way in DIRECTIONS:
                launch(functools.partial(make, z + way * d), valid(z + way * d))

    def each_source(step):
        for d in range(1, n):
            for way in DIRECTIONS:
                pl.when(valid(z - way * d))(functools.partial(step, z - way * d))

    def relay(take, give_on):
        def move(zb):
            take(zb).wait_recv()
            give_on(zb).start()

        each_source(move)
        for d in range(1, n):
            for way in DIRECTIONS:
                pending.append((functools.partial(give_on, z - way * d), valid(z - way * d)))

    def issue_weight(piece):
        issue(functools.partial(give_weight, piece))

    def relay_weight(piece):
        relay(functools.partial(take_weight, piece), functools.partial(pass_weight, piece))

    def finish_weight(piece):
        each_source(lambda zb: end_weight(piece, zb).wait_recv())

    def finish_tokens(d):
        for way in DIRECTIONS[: 1 if d == 0 else 2]:
            zb = z - way * d

            def finish(zb=zb):
                for k in range(2):
                    for xb in (x, 1 - x):
                        from_sibling(k, zb, xb).wait_recv()

            pl.when(valid(zb))(finish)

    def multiply_pair(h, zb):
        @pl.loop(0, 2)
        def _(k):
            top = pl.multiple_of(zb * rows, rows)
            to = pl.multiple_of(k * count + zb * rows, rows)
            p02[pl.ds(to, rows), :] = jnp.dot(
                full[k, pl.ds(top, rows), :], pairs[h], preferred_element_type=jnp.float32
            )

    def near(multiply, h, d):
        for way in DIRECTIONS[: 1 if d == 0 else 2]:
            pl.when(valid(z - way * d))(functools.partial(multiply, h, z - way * d))

    def multiply_rows(zb):
        @pl.loop(0, 2)
        def _(k):
            top = pl.multiple_of(zb * rows, rows)
            to = pl.multiple_of(k * count + zb * rows, rows)
            p1[pl.ds(to, rows), :] = jnp.dot(
                full[k, pl.ds(top, rows), :], mid[...], preferred_element_type=jnp.float32
            )

    def multiply_slice(h, zs, first):
        depth = pl.ds(pl.multiple_of(zs * deep, deep), deep)

        @pl.loop(0, 2 * n)
        def _(i):
            top = pl.multiple_of((i % n) * rows, rows)
            to = pl.ds(pl.multiple_of(i * rows, rows), rows)
            part = jnp.dot(
                full[i // n, pl.ds(top, rows), depth], pairs[h, depth, :],
                preferred_element_type=jnp.float32,
            )
            p02[to, :] = part if first else p02[to, :] + part

    line = lax.broadcasted_iota(jnp.int32, (count, half), 0)

    def forward(value, dst):
        high, low = split_value(value)
        xin[pl.ds(0, block), :] = high
        xin[pl.ds(block, block), :] = low
        xin[pl.ds(2 * block, block), :] = high

        @pl.loop(0, 2 * block // TILE)
        def _(m):
            at = pl.ds(pl.multiple_of(m * TILE, TILE), TILE)
            dst[at, :] = jnp.dot(table[at, :], xin[...], preferred_element_type=jnp.float32)

    def filter_spectra(h):
        lanes = pl.ds(h * half, half)
        for pair in range(blocks // 2):
            forward(
                jnp.concatenate(
                    [
                        ffull[pl.ds(2 * pair * block, block), lanes],
                        ffull[pl.ds((2 * pair + 1) * block, block), lanes],
                    ],
                    axis=1,
                ),
                plain.at[pair],
            )

        @pl.loop(0, 2 * block // STRIP)
        def _(m):
            at = pl.ds(pl.multiple_of(m * STRIP, STRIP), STRIP)
            row = lax.broadcasted_iota(jnp.int32, (STRIP, half), 0)
            sign = (1 - 2 * (row % 2)).astype(jnp.float32)
            before = None
            for b in range(blocks):
                left = (b % 2) * half
                here = plain[b // 2, at, left : left + half]
                kern[h, b, at, :] = here if before is None else here + sign * before
                before = here

    def filtered(ref, lanes, j, h, s):
        own_lanes = pl.ds(pl.multiple_of(z * own + h * half, half), half)
        value = ref[pl.ds(s * count, count), lanes]
        total = sw[0, pl.ds(j, 1), own_lanes] * value
        for o in range(1, taps):
            moved = jnp.where(line >= o, pltpu.roll(value, o, 0), 0.0)
            total = total + sw[o, pl.ds(j, 1), own_lanes] * moved
        return total

    def transform(h):
        low_lanes, high_lanes = pl.ds(0, half), pl.ds(half, half)
        first_gate = filtered(p02, low_lanes, 0, h, 0)
        second_gate = filtered(p02, high_lanes, 2, h, 0)
        gates[:, :half] = first_gate * second_gate
        gates[:, half:] = filtered(p02, low_lanes, 0, h, 1) * second_gate + first_gate * filtered(
            p02, high_lanes, 2, h, 1
        )
        for b in range(blocks):
            forward(gates[pl.ds(b * block, block), :], spec.at[b])

    def convolve(h):
        for b in range(blocks):

            @pl.loop(0, block // STRIP)
            def _(m):
                at = pl.ds(pl.multiple_of(m * STRIP, STRIP), STRIP)
                after = pl.ds(pl.multiple_of(block + m * STRIP, STRIP), STRIP)
                row = lax.broadcasted_iota(jnp.int32, (STRIP, 2 * half), 0) + m * STRIP
                first = row == 0
                weight = jnp.where(first, 0.5 / block, 1.0 / block)
                real, imag = 0.0, 0.0
                for a in range(b + 1):
                    kr, ki = kern[h, b - a, at, :], kern[h, b - a, after, :]
                    kr, ki = jnp.concatenate([kr, kr], axis=1), jnp.concatenate([ki, ki], axis=1)
                    vr, vi = spec[a, at, :], spec[a, after, :]
                    rr, ii = kr * vr, ki * vi
                    real = real + jnp.where(first, rr, rr - ii)
                    imag = imag + jnp.where(first, ii, kr * vi + ki * vr)
                for base, value in ((0, real), (block, imag)):
                    high, low = split_value(value * weight)
                    for third, part in enumerate((high, low, high)):
                        start = pl.multiple_of(third * 2 * block + base + m * STRIP, STRIP)
                        ycat[pl.ds(start, STRIP), :] = part

            @pl.loop(0, block // TILE)
            def _(m):
                at = pl.ds(pl.multiple_of(m * TILE, TILE), TILE)
                to = pl.ds(pl.multiple_of(b * block + m * TILE, TILE), TILE)
                conv[to, :] = jnp.dot(
                    inverse[at, :], ycat[...], preferred_element_type=jnp.float32
                )

    def give(h, o, target):
        top = pl.multiple_of(target * rows, rows)
        left = pl.multiple_of(z * own + h * half, half)
        return send(
            res.at[h, o, pl.ds(top, rows), :], outs[o].at[:, pl.ds(left, half)],
            send_sem.at[h, o, target], recv_sem.at[h, o, z], {"seq": target},
        )

    def take(h, o, source):
        top = pl.multiple_of(source * rows, rows)
        left = pl.multiple_of(source * own + h * half, half)
        return send(
            res.at[h, o, pl.ds(top, rows), :], outs[o].at[:, pl.ds(left, half)],
            send_sem.at[h, o, source], recv_sem.at[h, o, source], {"seq": source},
        )

    def keep(h, o):
        top = pl.multiple_of(z * rows, rows)
        left = pl.multiple_of(z * own + h * half, half)
        return pltpu.make_async_copy(
            res.at[h, o, pl.ds(top, rows), :], outs[o].at[:, pl.ds(left, half)], keep_sem.at[h, o]
        )

    def unit_place(h, o, source):
        left = pl.multiple_of(source * own + h * half, half)
        return units[o].at[:, pl.ds(left, half)]

    def give_unit(h, o, target):
        return send(
            top_of.at[h, target, o], unit_place(h, o, z),
            unit_send.at[h, o, target], unit_recv.at[h, o, z], {"seq": target},
        )

    def take_unit(h, o, source):
        return send(
            top_of.at[h, source, o], unit_place(h, o, source),
            unit_send.at[h, o, source], unit_recv.at[h, o, source], {"seq": source},
        )

    def keep_unit(h, o):
        return pltpu.make_async_copy(
            top_of.at[h, z, o], unit_place(h, o, z), unit_keep.at[h, o]
        )

    def answer(h):
        mids[:, :half] = filtered(p1, pl.ds(h * half, half), 1, h, 0)
        mids[:, half:] = filtered(p1, pl.ds(h * half, half), 1, h, 1)
        gain = skip[:, pl.ds(pl.multiple_of(z * own + h * half, half), half)]

        @pl.loop(0, n)
        def _(i):
            target = jnp.where(z < n // 2, n - 1 - i, i)

            def values(m, most):
                at = pl.ds(pl.multiple_of(target * rows + m * STRIP, STRIP), STRIP)
                combined = conv[at, :half] + gain * gates[at, :half]
                dcombined = conv[at, half:] + gain * gates[at, half:]
                middle = mids[at, :half]
                first = middle * combined
                second = mids[at, half:] * combined + middle * dcombined
                here = pl.ds(pl.multiple_of(m * STRIP, STRIP), STRIP)
                raw[0, here, :] = first
                raw[1, here, :] = second
                return tuple(
                    jnp.maximum(old, jnp.max(jnp.abs(new).reshape(STRIP // 8, 8, half), axis=0))
                    for old, new in zip(most, (first, second))
                )

            nothing = jnp.zeros((8, half), jnp.float32)
            most = lax.fori_loop(0, rows // STRIP, values, (nothing, nothing))
            for o in range(2):
                peak = jnp.maximum(jnp.max(most[o], axis=0, keepdims=True), TINY)
                top_of[h, target, o] = jnp.broadcast_to(peak * (1.0 / REACH), (8, half))
                scale = REACH / peak

                @pl.loop(0, rows // STRIP)
                def _(m):
                    here = pl.ds(pl.multiple_of(m * STRIP, STRIP), STRIP)
                    at = pl.ds(pl.multiple_of(target * rows + m * STRIP, STRIP), STRIP)
                    res[h, o, at, :] = encode(raw[o, here, :] * scale)

            @pl.when(target != z)
            def _():
                for o in range(2):
                    give_unit(h, o, target).start()
                    give(h, o, target).start()

        for o in range(2):
            keep_unit(h, o).start()
            keep(h, o).start()

    def issue_filter():
        issue(give_filter)

    def relay_filter():
        relay(take_filter, pass_filter)

    first_pair, second_pair = ((0, 0), (2, 0)), ((0, 1), (2, 1))
    first_mid, second_mid = (1, 0), (1, 1)

    relay_column(1)
    issue_filter()
    for piece in (*first_pair, first_mid):
        issue_weight(piece)
    relay_across(0)
    relay_column(2)
    relay_across(1)
    relay_filter()
    relay_weight(first_pair[0])
    issue_weight(second_mid)
    relay_weight(first_pair[1])
    relay_weight(first_mid)
    issue_weight(second_pair[0])
    for copy in locals_:
        copy.wait()
    each_source(lambda zb: end_filter(zb).wait_recv())
    for h in range(2):
        filter_spectra(h)
    for piece in first_pair:
        finish_weight(piece)
    for d in range(2):
        finish_tokens(d)
        near(multiply_pair, 0, d)
    for d in range(3, n):
        relay_column(d)
    relay_across(2)
    relay_weight(second_mid)
    issue_weight(second_pair[1])
    finish_tokens(2)
    near(multiply_pair, 0, 2)
    for d in range(3, n):
        relay_across(d)
        finish_tokens(d)
        near(multiply_pair, 0, d)
    transform(0)
    relay_weight(second_pair[0])
    convolve(0)
    finish_weight(first_mid)
    finish_weight(second_mid)

    @pl.loop(0, n)
    def _(zb):
        multiply_rows(zb)

    relay_weight(second_pair[1])
    answer(0)
    finish_weight(second_pair[0])
    multiply_slice(1, z, True)

    def source(i):
        return jnp.where(z < n // 2, lax.rem(z + i, n), lax.rem(z + n - i, n))

    for i in range(1, n):
        end_weight(second_pair[1], source(i)).wait_recv()
        multiply_slice(1, source(i), False)
    transform(1)
    convolve(1)
    answer(1)

    for make, condition in pending:
        if condition is None:
            make().wait_send()
        else:
            pl.when(condition)(lambda make=make: make().wait_send())
    for h in range(2):
        for o in range(2):
            keep_unit(h, o).wait()
            keep(h, o).wait()
        for d in range(1, n):
            for way in DIRECTIONS:
                there = z + way * d

                def finish(h=h, there=there):
                    for o in range(2):
                        take_unit(h, o, there).wait_recv()
                        give_unit(h, o, there).wait_send()
                        take(h, o, there).wait_recv()
                        give(h, o, there).wait_send()

                pl.when(valid(there))(finish)


def hyena(tokens, tangent, wt, long_filter, short_weight, skip_gain, block):
    n = lax.axis_size("seq")
    rows, wide = tokens.shape
    own = wt.shape[2] // n
    half, count = own // 2, rows * n
    blocks = count // block
    table = dft_table(block)
    vmem = pl.BlockSpec(memory_space=pltpu.VMEM)
    anywhere = pl.BlockSpec(memory_space=pl.ANY)
    sem = pltpu.SemaphoreType.DMA
    f32, bf16 = jnp.float32, jnp.bfloat16
    shape = jax.ShapeDtypeStruct((rows, own * n), bf16)
    first, second, unit0, unit1 = pl.pallas_call(
        functools.partial(hyena_kernel, n, block),
        out_shape=(shape, shape) + (jax.ShapeDtypeStruct((8, own * n), f32),) * 2,
        in_specs=[anywhere] * 4 + [vmem] * 2 + [anywhere] * 2,
        out_specs=(anywhere,) * 4,
        scratch_shapes=[
            pltpu.VMEM((2, count, wide * 4), bf16),
            pltpu.VMEM((2, wt.shape[1] * n, own), bf16),
            pltpu.VMEM((wt.shape[1] * n, own), bf16),
            pltpu.VMEM((count, own), f32),
            pltpu.VMEM((2 * block, 3 * block), bf16),
            pltpu.VMEM((block, 6 * block), bf16),
            pltpu.VMEM((2 * count, own), f32),
            pltpu.VMEM((2 * count, own), f32),
            pltpu.VMEM((count, own), f32),
            pltpu.VMEM((count, own), f32),
            pltpu.VMEM((3 * block, own), bf16),
            pltpu.VMEM((blocks, 2 * block, own), f32),
            pltpu.VMEM((blocks // 2, 2 * block, own), f32),
            pltpu.VMEM((2, blocks, 2 * block, half), f32),
            pltpu.VMEM((6 * block, own), bf16),
            pltpu.VMEM((count, own), f32),
            pltpu.VMEM((2, rows, half), f32),
            pltpu.VMEM((2, 2, count, half), bf16),
            pltpu.VMEM((2, n, 2, 8, half), f32),
            sem((5,)), sem((6,)),
            sem((2, n, 2)), sem((2, n)), sem((2, n)), sem((2, n)), sem((2, 2, n)), sem((2, 2, n)),
            sem((6, n)), sem((6, n)), sem((6, n)), sem((6, n)), sem((n,)), sem((n,)), sem((n,)), sem((n,)),
            sem((2, 2, n)), sem((2, 2, n)), sem((2, 2)),
            sem((2, 2, n)), sem((2, 2, n)), sem((2, 2)),
        ],
        compiler_params=pltpu.CompilerParams(
            collective_id=0, has_side_effects=True, vmem_limit_bytes=60 * 2**20
        ),
        name="hyena",
    )(
        tokens, tangent, wt, long_filter, short_weight, skip_gain.reshape(1, -1),
        jnp.asarray(split_table(table, 1)), jnp.asarray(split_table(table.T, 1)),
    )
    return decode(first, unit0), decode(second, unit1)


def body(tokens, tangent, in_weight, short_weight, long_filter, skip_gain):
    devices = lax.axis_size("seq")
    shard = lax.axis_index("seq")
    own = in_weight.shape[2] // devices
    wt = in_weight.transpose(1, 0, 2)
    by_copies = own == 256 and devices == 4 and all(lax.axis_size(axis) == 2 for axis in ("grp", "chan", "sub"))
    block = min(512, long_filter.shape[0] * devices)
    if by_copies:
        return hyena(tokens, tangent, wt, long_filter, short_weight, skip_gain, block)

    both = jnp.stack([tokens, tangent])
    both = lax.all_gather(both, ("chan", "sub"), axis=2, tiled=True)
    both = lax.all_gather(both, "seq", axis=1, tiled=True)
    weight = lax.all_to_all(wt, "seq", split_axis=2, concat_axis=1, tiled=True)
    long_filter = lax.all_to_all(long_filter, "seq", split_axis=1, concat_axis=0, tiled=True)
    short_weight = lax.dynamic_slice_in_dim(short_weight, shard * own, own, axis=2)
    skip_gain = lax.dynamic_slice_in_dim(skip_gain, shard * own, own, axis=0)

    def project(values):
        return [jnp.dot(values, weight[j], preferred_element_type=jnp.float32) for j in range(3)]

    proj, dproj = project(both[0]), project(both[1])
    outs = operator(proj, dproj, short_weight, long_filter, skip_gain, block)
    return tuple(
        lax.all_to_all(value, "seq", split_axis=0, concat_axis=1, tiled=True) for value in outs
    )


def solution(mesh):
    placed = (
        P(("grp", "seq"), ("chan", "sub")),
        P(("grp", "seq"), ("chan", "sub")),
        P("seq", None, ("chan", "sub")),
        P(None, None, ("chan", "sub")),
        P("seq", ("chan", "sub")),
        P(("chan", "sub")),
    )
    return jax.shard_map(
        body,
        mesh=mesh,
        in_specs=placed,
        out_specs=(P(("grp", "seq"), ("chan", "sub")), P(("grp", "seq"), ("chan", "sub"))),
        check_vma=False,
    )
```

```python
import functools
import math

import jax
import jax.numpy as jnp
import numpy as np
from jax import lax
from jax.experimental import pallas as pl
from jax.experimental.pallas import tpu as pltpu
from jax.sharding import PartitionSpec as P

HIGH = lax.Precision.HIGH


def dft_table(block):
    size = 2 * block
    freqs = np.arange(block)[:, None]
    times = np.arange(block)[None, :]
    theta = (freqs * times % size) * (2.0 * math.pi / size)
    cosine = np.cos(theta)
    sine = -np.sin(theta)
    sine[0] = 1.0 - 2.0 * (np.arange(block) % 2)
    return np.concatenate([cosine, sine], axis=0).astype(np.float32)


def causal_convs(signals, long_filter, block):
    count = long_filter.shape[0]
    blocks = count // block
    table = jnp.asarray(dft_table(block))
    index = lax.broadcasted_iota(jnp.int32, (block, 1), 0)
    first = index == 0
    sign = (1 - 2 * (index % 2)).astype(jnp.float32)
    weight = jnp.where(first, 0.5 / block, 1.0 / block).astype(jnp.float32)

    def spectra(values):
        result = []
        for b in range(blocks):
            both = jnp.dot(table, values[b * block : (b + 1) * block], precision=HIGH)
            result.append((both[:block], both[block:]))
        return result

    plain = spectra(long_filter)
    kernels = [plain[0]]
    for b in range(1, blocks):
        kernels.append(tuple(here + sign * before for here, before in zip(plain[b], plain[b - 1])))
    outs = []
    for values in signals:
        moved = spectra(values)
        rows = []
        for b in range(blocks):
            real, imag = 0.0, 0.0
            for a in range(b + 1):
                kr, ki = kernels[b - a]
                vr, vi = moved[a]
                rr, ii = kr * vr, ki * vi
                real = real + jnp.where(first, rr, rr - ii)
                imag = imag + jnp.where(first, ii, kr * vi + ki * vr)
            packed = jnp.concatenate([real * weight, imag * weight], axis=0)
            rows.append(
                lax.dot_general(table, packed, (((0,), (0,)), ((), ())), precision=HIGH)
            )
        outs.append(jnp.concatenate(rows, axis=0))
    return outs


def short_filter(values, weights):
    count = values.shape[0]
    total = weights[0] * values
    for offset in range(1, weights.shape[0]):
        total = total + weights[offset] * jnp.pad(values, ((offset, 0), (0, 0)))[:count]
    return total


def operator(proj, dproj, short_weight, long_filter, skip_gain, block):
    mixed = [short_filter(proj[j], short_weight[:, j]) for j in range(3)]
    dmixed = [short_filter(dproj[j], short_weight[:, j]) for j in range(3)]
    gated_in = mixed[0] * mixed[2]
    dgated_in = dmixed[0] * mixed[2] + mixed[0] * dmixed[2]
    conv, dconv = causal_convs((gated_in, dgated_in), long_filter, block)
    combined = conv + skip_gain * gated_in
    dcombined = dconv + skip_gain * dgated_in
    return mixed[1] * combined, dmixed[1] * combined + mixed[1] * dcombined

MESH = pl.DeviceIdType.MESH
DIRECTIONS = (1, -1)


def split_table(table, axis):
    high = table.astype(jnp.bfloat16)
    low = (table - high.astype(np.float32)).astype(jnp.bfloat16)
    return np.concatenate([high, high, low], axis=axis)


def split_value(value):
    high = value.astype(jnp.bfloat16)
    return high, (value - high.astype(jnp.float32)).astype(jnp.bfloat16)


TILE = 256
STRIP = 64
POWER = 12
REACH = 1400.0
TINY = 1e-34


def encode(value):
    second = value * value
    fourth = second * second
    code = fourth * fourth * fourth
    return jnp.where(value < 0, -code, code).astype(jnp.bfloat16)


def decode(code, unit):
    value = code.astype(jnp.float32).reshape(-1, *unit.shape)
    size = jnp.exp2(jnp.log2(jnp.abs(value)) * (1.0 / POWER)) * unit
    return jnp.where(value > 0, size, jnp.where(value < 0, -size, 0.0)).reshape(code.shape)


def hyena_kernel(
    n, block, tok, tan, wt, filt, sw, skip, table_in, inverse_in, out0, out1, unit0, unit1,
    full, pairs, mid, ffull, fin, fown, uown, fcode, funit, table, inverse, p02, p1,
    gates, mids, xin, spec, plain, kern, ycat, conv, raw, res, top_of,
    local_sem, own_sem, col_send, col_recv, x_send, x_recv, c_send, c_recv,
    w_send, w_recv, y_send, y_recv, f_send, f_recv, fy_send, fy_recv, u_send, u_recv,
    send_sem, recv_sem, keep_sem, unit_send, unit_recv, unit_keep,
):
    g, z = lax.axis_index("grp"), lax.axis_index("seq")
    x, c = lax.axis_index("chan"), lax.axis_index("sub")
    rows, wide = tok.shape
    count = rows * n
    deep, own = wt.shape[1], wt.shape[2] // n
    half, deep2, fhalf = own // 2, deep // 2, filt.shape[0] // 2
    blocks = count // block
    taps = sw.shape[0]
    sources = (tok, tan)
    outs = (out0, out1)
    units = (unit0, unit1)
    pending = []

    def valid(place):
        return jnp.logical_and(place >= 0, place < n)

    def send(src, dst, send_sem, recv_sem, where):
        return pltpu.make_async_remote_copy(
            src_ref=src, dst_ref=dst, send_sem=send_sem, recv_sem=recv_sem,
            device_id=where, device_id_type=MESH,
        )

    def slot(k, zb, xb, cb):
        top = pl.multiple_of(zb * rows, rows)
        left = pl.multiple_of((xb * 2 + cb) * wide, wide)
        return full.at[k, pl.ds(top, rows), pl.ds(left, wide)]

    def column(k, zb, way, first):
        dst = slot(k, zb, x, c)
        src = sources[k] if first else dst
        lane = 0 if way > 0 else 1
        return send(src, dst, col_send.at[k, zb, lane], col_recv.at[k, zb], {"seq": z + way})

    def across(k, zb, first):
        dst = slot(k, zb, x, c)
        src = sources[k] if first else dst
        return send(src, dst, x_send.at[k, zb], x_recv.at[k, zb], {"chan": 1 - x})

    def sibling(k, zb, other, first):
        xb = 1 - x if other else x
        dst = slot(k, zb, xb, c)
        src = sources[k] if first else dst
        return send(src, dst, c_send.at[k, xb, zb], c_recv.at[k, xb, zb], {"sub": 1 - c})

    def from_sibling(k, zb, xb):
        dst = slot(k, zb, xb, 1 - c)
        return send(dst, dst, c_send.at[k, xb, zb], c_recv.at[k, xb, zb], {"sub": 1 - c})

    def from_across(k, zb):
        dst = slot(k, zb, 1 - x, c)
        return send(dst, dst, x_send.at[k, zb], x_recv.at[k, zb], {"chan": 1 - x})

    def weight_rows(piece, top, size):
        j, h = piece
        if j == 1:
            return mid.at[pl.ds(top, size), pl.ds(h * half, half)]
        return pairs.at[h, pl.ds(top, size), pl.ds((j // 2) * half, half)]

    def weight_part(piece, zb, gb):
        return weight_rows(piece, pl.multiple_of(zb * deep + gb * deep2, deep2), deep2)

    def filter_part(zb, gb):
        top = pl.multiple_of(zb * 2 * fhalf + gb * fhalf, fhalf)
        return fcode.at[pl.ds(top, fhalf), :]

    def number(piece):
        return piece[0] * 2 + piece[1]

    def give_weight(piece, target):
        left = pl.multiple_of(target * own + piece[1] * half, half)
        top = pl.multiple_of(g * deep2, deep2)
        src = wt.at[piece[0], pl.ds(top, deep2), pl.ds(left, half)]
        q = number(piece)
        return send(
            src, weight_part(piece, z, g), w_send.at[q, target], w_recv.at[q, z], {"seq": target}
        )

    def give_filter(target):
        left = pl.multiple_of(target * own, own)
        top = pl.multiple_of(g * fhalf, fhalf)
        src = fown.at[pl.ds(top, fhalf), pl.ds(left, own)]
        return send(src, filter_part(z, g), f_send.at[target], f_recv.at[z], {"seq": target})

    def give_scale(target):
        src = uown.at[:, pl.ds(pl.multiple_of(target * own, own), own)]
        return send(src, funit.at[z], u_send.at[target], u_recv.at[z], {"seq": target})

    def take_scale(zb):
        return send(funit.at[zb], funit.at[zb], u_send.at[zb], u_recv.at[zb], {"seq": zb})

    def take_weight(piece, zb):
        ref, q = weight_part(piece, zb, g), number(piece)
        return send(ref, ref, w_send.at[q, zb], w_recv.at[q, zb], {"seq": zb})

    def take_filter(zb):
        ref = filter_part(zb, g)
        return send(ref, ref, f_send.at[zb], f_recv.at[zb], {"seq": zb})

    def pass_weight(piece, zb):
        ref, q = weight_part(piece, zb, g), number(piece)
        return send(ref, ref, y_send.at[q, zb], y_recv.at[q, zb], {"grp": 1 - g})

    def pass_filter(zb):
        ref = filter_part(zb, g)
        return send(ref, ref, fy_send.at[zb], fy_recv.at[zb], {"grp": 1 - g})

    def end_weight(piece, zb):
        ref, q = weight_part(piece, zb, 1 - g), number(piece)
        return send(ref, ref, y_send.at[q, zb], y_recv.at[q, zb], {"grp": 1 - g})

    def end_filter(zb):
        ref = filter_part(zb, 1 - g)
        return send(ref, ref, fy_send.at[zb], fy_recv.at[zb], {"grp": 1 - g})

    barrier = pltpu.get_barrier_semaphore()
    for d in range(1, n):
        for way in DIRECTIONS:
            there = z + way * d

            @pl.when(valid(there))
            def _():
                pl.semaphore_signal(barrier, inc=1, device_id={"seq": there}, device_id_type=MESH)

    for where in ({"chan": 1 - x}, {"grp": 1 - g}, {"sub": 1 - c}):
        pl.semaphore_signal(barrier, inc=1, device_id=where, device_id_type=MESH)
    pl.semaphore_wait(barrier, n + 2)

    def launch(make, condition=None):
        pending.append((make, condition))
        if condition is None:
            make().start()
        else:
            pl.when(condition)(lambda: make().start())

    for k in range(2):
        for way in DIRECTIONS:
            launch(functools.partial(column, k, z, way, True), valid(z + way))
        launch(functools.partial(across, k, z, True))
        launch(functools.partial(sibling, k, z, False, True))
    mine = pl.ds(pl.multiple_of(z * own, own), own)
    locals_ = [
        pltpu.make_async_copy(tok, slot(0, z, x, c), local_sem.at[0]),
        pltpu.make_async_copy(tan, slot(1, z, x, c), local_sem.at[1]),
        pltpu.make_async_copy(table_in, table, local_sem.at[3]),
        pltpu.make_async_copy(inverse_in, inverse, local_sem.at[4]),
    ]
    for j in range(3):
        for h in range(2):
            piece = (j, h)
            left = pl.multiple_of(z * own + h * half, half)
            locals_.append(
                pltpu.make_async_copy(
                    wt.at[j, :, pl.ds(left, half)],
                    weight_rows(piece, pl.multiple_of(z * deep, deep), deep),
                    own_sem.at[number(piece)],
                )
            )
    for copy in locals_:
        copy.start()
    fetch = pltpu.make_async_copy(filt, fin, local_sem.at[2])
    fetch.start()
    fetch.wait()

    def highest(m, most):
        at = pl.ds(pl.multiple_of(m * STRIP, STRIP), STRIP)
        size = jnp.abs(fin[at, :]).reshape(STRIP // 8, 8, own * n)
        return jnp.maximum(most, jnp.max(size, axis=0))

    most = lax.fori_loop(0, 2 * fhalf // STRIP, highest, jnp.zeros((8, own * n), jnp.float32))
    peak = jnp.maximum(jnp.max(most, axis=0, keepdims=True), TINY)
    uown[...] = jnp.broadcast_to(peak * (1.0 / REACH), (8, own * n))
    scale = REACH / peak

    @pl.loop(0, 2 * fhalf // STRIP)
    def _(m):
        at = pl.ds(pl.multiple_of(m * STRIP, STRIP), STRIP)
        fown[at, :] = encode(fin[at, :] * scale)

    own_filter = [
        pltpu.make_async_copy(
            fown.at[:, mine],
            fcode.at[pl.ds(pl.multiple_of(z * 2 * fhalf, 2 * fhalf), 2 * fhalf), :],
            own_sem.at[6],
        ),
        pltpu.make_async_copy(uown.at[:, mine], funit.at[z], own_sem.at[7]),
    ]
    for copy in own_filter:
        copy.start()
    locals_ = locals_ + own_filter

    def relay_across(d):
        for k in range(2):
            for way in DIRECTIONS[: 1 if d == 0 else 2]:
                zb = z - way * d

                def step(k=k, zb=zb):
                    from_across(k, zb).wait_recv()
                    sibling(k, zb, True, False).start()

                pending.append((functools.partial(sibling, k, zb, True, False), valid(zb)))
                pl.when(valid(zb))(step)

    def relay_column(d):
        for k in range(2):
            for way in DIRECTIONS:
                zb = z - way * d
                on = jnp.logical_and(valid(zb), valid(z + way))

                def arrive(k=k, zb=zb, way=way):
                    column(k, zb, way, False).wait_recv()

                def after(k=k, zb=zb):
                    across(k, zb, False).start()
                    sibling(k, zb, False, False).start()

                pl.when(valid(zb))(arrive)
                launch(functools.partial(column, k, zb, way, False), on)
                pl.when(valid(zb))(after)
                pending.append((functools.partial(across, k, zb, False), valid(zb)))
                pending.append((functools.partial(sibling, k, zb, False, False), valid(zb)))

    def issue(make):
        for d in range(1, n):
            for way in DIRECTIONS:
                launch(functools.partial(make, z + way * d), valid(z + way * d))

    def each_source(step):
        for d in range(1, n):
            for way in DIRECTIONS:
                pl.when(valid(z - way * d))(functools.partial(step, z - way * d))

    def relay(take, give_on):
        def move(zb):
            take(zb).wait_recv()
            give_on(zb).start()

        each_source(move)
        for d in range(1, n):
            for way in DIRECTIONS:
                pending.append((functools.partial(give_on, z - way * d), valid(z - way * d)))

    def issue_weight(piece):
        issue(functools.partial(give_weight, piece))

    def relay_weight(piece):
        relay(functools.partial(take_weight, piece), functools.partial(pass_weight, piece))

    def finish_weight(piece):
        each_source(lambda zb: end_weight(piece, zb).wait_recv())

    def finish_tokens(d):
        for way in DIRECTIONS[: 1 if d == 0 else 2]:
            zb = z - way * d

            def finish(zb=zb):
                for k in range(2):
                    for xb in (x, 1 - x):
                        from_sibling(k, zb, xb).wait_recv()

            pl.when(valid(zb))(finish)

    def multiply_pair(h, zb):
        @pl.loop(0, 2)
        def _(k):
            top = pl.multiple_of(zb * rows, rows)
            to = pl.multiple_of(k * count + zb * rows, rows)
            p02[pl.ds(to, rows), :] = jnp.dot(
                full[k, pl.ds(top, rows), :], pairs[h], preferred_element_type=jnp.float32
            )

    def near(multiply, h, d):
        for way in DIRECTIONS[: 1 if d == 0 else 2]:
            pl.when(valid(z - way * d))(functools.partial(multiply, h, z - way * d))

    def multiply_rows(zb):
        @pl.loop(0, 2)
        def _(k):
            top = pl.multiple_of(zb * rows, rows)
            to = pl.multiple_of(k * count + zb * rows, rows)
            p1[pl.ds(to, rows), :] = jnp.dot(
                full[k, pl.ds(top, rows), :], mid[...], preferred_element_type=jnp.float32
            )

    def multiply_slice(h, zs, first):
        depth = pl.ds(pl.multiple_of(zs * deep, deep), deep)

        @pl.loop(0, 2 * n)
        def _(i):
            top = pl.multiple_of((i % n) * rows, rows)
            to = pl.ds(pl.multiple_of(i * rows, rows), rows)
            part = jnp.dot(
                full[i // n, pl.ds(top, rows), depth], pairs[h, depth, :],
                preferred_element_type=jnp.float32,
            )
            p02[to, :] = part if first else p02[to, :] + part

    line = lax.broadcasted_iota(jnp.int32, (count, half), 0)

    def forward(value, dst):
        high, low = split_value(value)
        xin[pl.ds(0, block), :] = high
        xin[pl.ds(block, block), :] = low
        xin[pl.ds(2 * block, block), :] = high

        @pl.loop(0, 2 * block // TILE)
        def _(m):
            at = pl.ds(pl.multiple_of(m * TILE, TILE), TILE)
            dst[at, :] = jnp.dot(table[at, :], xin[...], preferred_element_type=jnp.float32)

    def filter_spectra(h):
        lanes = pl.ds(h * half, half)
        for pair in range(blocks // 2):
            forward(
                jnp.concatenate(
                    [
                        ffull[pl.ds(2 * pair * block, block), lanes],
                        ffull[pl.ds((2 * pair + 1) * block, block), lanes],
                    ],
                    axis=1,
                ),
                plain.at[pair],
            )

        @pl.loop(0, 2 * block // STRIP)
        def _(m):
            at = pl.ds(pl.multiple_of(m * STRIP, STRIP), STRIP)
            row = lax.broadcasted_iota(jnp.int32, (STRIP, half), 0)
            sign = (1 - 2 * (row % 2)).astype(jnp.float32)
            before = None
            for b in range(blocks):
                left = (b % 2) * half
                here = plain[b // 2, at, left : left + half]
                kern[h, b, at, :] = here if before is None else here + sign * before
                before = here

    def filtered(ref, lanes, j, h, s):
        own_lanes = pl.ds(pl.multiple_of(z * own + h * half, half), half)
        value = ref[pl.ds(s * count, count), lanes]
        total = sw[0, pl.ds(j, 1), own_lanes] * value
        for o in range(1, taps):
            moved = jnp.where(line >= o, pltpu.roll(value, o, 0), 0.0)
            total = total + sw[o, pl.ds(j, 1), own_lanes] * moved
        return total

    def transform(h):
        low_lanes, high_lanes = pl.ds(0, half), pl.ds(half, half)
        first_gate = filtered(p02, low_lanes, 0, h, 0)
        second_gate = filtered(p02, high_lanes, 2, h, 0)
        gates[:, :half] = first_gate * second_gate
        gates[:, half:] = filtered(p02, low_lanes, 0, h, 1) * second_gate + first_gate * filtered(
            p02, high_lanes, 2, h, 1
        )
        for b in range(blocks):
            forward(gates[pl.ds(b * block, block), :], spec.at[b])

    def convolve(h):
        for b in range(blocks):

            @pl.loop(0, block // STRIP)
            def _(m):
                at = pl.ds(pl.multiple_of(m * STRIP, STRIP), STRIP)
                after = pl.ds(pl.multiple_of(block + m * STRIP, STRIP), STRIP)
                row = lax.broadcasted_iota(jnp.int32, (STRIP, 2 * half), 0) + m * STRIP
                first = row == 0
                weight = jnp.where(first, 0.5 / block, 1.0 / block)
                real, imag = 0.0, 0.0
                for a in range(b + 1):
                    kr, ki = kern[h, b - a, at, :], kern[h, b - a, after, :]
                    kr, ki = jnp.concatenate([kr, kr], axis=1), jnp.concatenate([ki, ki], axis=1)
                    vr, vi = spec[a, at, :], spec[a, after, :]
                    rr, ii = kr * vr, ki * vi
                    real = real + jnp.where(first, rr, rr - ii)
                    imag = imag + jnp.where(first, ii, kr * vi + ki * vr)
                for base, value in ((0, real), (block, imag)):
                    high, low = split_value(value * weight)
                    for third, part in enumerate((high, low, high)):
                        start = pl.multiple_of(third * 2 * block + base + m * STRIP, STRIP)
                        ycat[pl.ds(start, STRIP), :] = part

            @pl.loop(0, block // TILE)
            def _(m):
                at = pl.ds(pl.multiple_of(m * TILE, TILE), TILE)
                to = pl.ds(pl.multiple_of(b * block + m * TILE, TILE), TILE)
                conv[to, :] = jnp.dot(
                    inverse[at, :], ycat[...], preferred_element_type=jnp.float32
                )

    def give(h, o, target):
        top = pl.multiple_of(target * rows, rows)
        left = pl.multiple_of(z * own + h * half, half)
        return send(
            res.at[h, o, pl.ds(top, rows), :], outs[o].at[:, pl.ds(left, half)],
            send_sem.at[h, o, target], recv_sem.at[h, o, z], {"seq": target},
        )

    def take(h, o, source):
        top = pl.multiple_of(source * rows, rows)
        left = pl.multiple_of(source * own + h * half, half)
        return send(
            res.at[h, o, pl.ds(top, rows), :], outs[o].at[:, pl.ds(left, half)],
            send_sem.at[h, o, source], recv_sem.at[h, o, source], {"seq": source},
        )

    def keep(h, o):
        top = pl.multiple_of(z * rows, rows)
        left = pl.multiple_of(z * own + h * half, half)
        return pltpu.make_async_copy(
            res.at[h, o, pl.ds(top, rows), :], outs[o].at[:, pl.ds(left, half)], keep_sem.at[h, o]
        )

    def unit_place(h, o, source):
        left = pl.multiple_of(source * own + h * half, half)
        return units[o].at[:, pl.ds(left, half)]

    def give_unit(h, o, target):
        return send(
            top_of.at[h, target, o], unit_place(h, o, z),
            unit_send.at[h, o, target], unit_recv.at[h, o, z], {"seq": target},
        )

    def take_unit(h, o, source):
        return send(
            top_of.at[h, source, o], unit_place(h, o, source),
            unit_send.at[h, o, source], unit_recv.at[h, o, source], {"seq": source},
        )

    def keep_unit(h, o):
        return pltpu.make_async_copy(
            top_of.at[h, z, o], unit_place(h, o, z), unit_keep.at[h, o]
        )

    def answer(h):
        mids[:, :half] = filtered(p1, pl.ds(h * half, half), 1, h, 0)
        mids[:, half:] = filtered(p1, pl.ds(h * half, half), 1, h, 1)
        gain = skip[:, pl.ds(pl.multiple_of(z * own + h * half, half), half)]

        @pl.loop(0, n)
        def _(i):
            target = jnp.where(z < n // 2, n - 1 - i, i)

            def values(m, most):
                at = pl.ds(pl.multiple_of(target * rows + m * STRIP, STRIP), STRIP)
                combined = conv[at, :half] + gain * gates[at, :half]
                dcombined = conv[at, half:] + gain * gates[at, half:]
                middle = mids[at, :half]
                first = middle * combined
                second = mids[at, half:] * combined + middle * dcombined
                here = pl.ds(pl.multiple_of(m * STRIP, STRIP), STRIP)
                raw[0, here, :] = first
                raw[1, here, :] = second
                return tuple(
                    jnp.maximum(old, jnp.max(jnp.abs(new).reshape(STRIP // 8, 8, half), axis=0))
                    for old, new in zip(most, (first, second))
                )

            nothing = jnp.zeros((8, half), jnp.float32)
            most = lax.fori_loop(0, rows // STRIP, values, (nothing, nothing))
            for o in range(2):
                peak = jnp.maximum(jnp.max(most[o], axis=0, keepdims=True), TINY)
                top_of[h, target, o] = jnp.broadcast_to(peak * (1.0 / REACH), (8, half))
                scale = REACH / peak

                @pl.loop(0, rows // STRIP)
                def _(m):
                    here = pl.ds(pl.multiple_of(m * STRIP, STRIP), STRIP)
                    at = pl.ds(pl.multiple_of(target * rows + m * STRIP, STRIP), STRIP)
                    res[h, o, at, :] = encode(raw[o, here, :] * scale)

            @pl.when(target != z)
            def _():
                for o in range(2):
                    give_unit(h, o, target).start()
                    give(h, o, target).start()

        for o in range(2):
            keep_unit(h, o).start()
            keep(h, o).start()

    def issue_filter():
        issue(give_scale)
        issue(give_filter)

    def relay_filter():
        relay(take_filter, pass_filter)

    first_pair, second_pair = ((0, 0), (2, 0)), ((0, 1), (2, 1))
    first_mid, second_mid = (1, 0), (1, 1)

    relay_column(1)
    issue_filter()
    for piece in (*first_pair, first_mid):
        issue_weight(piece)
    relay_across(0)
    relay_column(2)
    relay_across(1)
    relay_filter()
    relay_weight(first_pair[0])
    issue_weight(second_mid)
    relay_weight(first_pair[1])
    relay_weight(first_mid)
    issue_weight(second_pair[0])
    for copy in locals_:
        copy.wait()
    each_source(lambda zb: end_filter(zb).wait_recv())
    each_source(lambda zb: take_scale(zb).wait_recv())

    @pl.loop(0, count // STRIP)
    def _(m):
        at = pl.ds(pl.multiple_of(m * STRIP, STRIP), STRIP)
        ffull[at, :] = decode(fcode[at, :], funit[m // (2 * fhalf // STRIP)])

    for h in range(2):
        filter_spectra(h)
    for piece in first_pair:
        finish_weight(piece)
    for d in range(2):
        finish_tokens(d)
        near(multiply_pair, 0, d)
    for d in range(3, n):
        relay_column(d)
    relay_across(2)
    relay_weight(second_mid)
    issue_weight(second_pair[1])
    finish_tokens(2)
    near(multiply_pair, 0, 2)
    relay_weight(second_pair[0])
    for d in range(3, n):
        relay_across(d)
        finish_tokens(d)
        near(multiply_pair, 0, d)
    transform(0)
    convolve(0)
    relay_weight(second_pair[1])
    finish_weight(first_mid)
    finish_weight(second_mid)

    @pl.loop(0, n)
    def _(zb):
        multiply_rows(zb)

    answer(0)
    finish_weight(second_pair[0])
    multiply_slice(1, z, True)

    def source(i):
        return jnp.where(z < n // 2, lax.rem(z + i, n), lax.rem(z + n - i, n))

    for i in range(1, n):
        end_weight(second_pair[1], source(i)).wait_recv()
        multiply_slice(1, source(i), False)
    transform(1)
    convolve(1)
    answer(1)

    for make, condition in pending:
        if condition is None:
            make().wait_send()
        else:
            pl.when(condition)(lambda make=make: make().wait_send())
    for h in range(2):
        for o in range(2):
            keep_unit(h, o).wait()
            keep(h, o).wait()
        for d in range(1, n):
            for way in DIRECTIONS:
                there = z + way * d

                def finish(h=h, there=there):
                    for o in range(2):
                        take_unit(h, o, there).wait_recv()
                        give_unit(h, o, there).wait_send()
                        take(h, o, there).wait_recv()
                        give(h, o, there).wait_send()

                pl.when(valid(there))(finish)


def hyena(tokens, tangent, wt, long_filter, short_weight, skip_gain, block):
    n = lax.axis_size("seq")
    rows, wide = tokens.shape
    own = wt.shape[2] // n
    half, count = own // 2, rows * n
    blocks = count // block
    table = dft_table(block)
    vmem = pl.BlockSpec(memory_space=pltpu.VMEM)
    anywhere = pl.BlockSpec(memory_space=pl.ANY)
    sem = pltpu.SemaphoreType.DMA
    f32, bf16 = jnp.float32, jnp.bfloat16
    shape = jax.ShapeDtypeStruct((rows, own * n), bf16)
    first, second, unit0, unit1 = pl.pallas_call(
        functools.partial(hyena_kernel, n, block),
        out_shape=(shape, shape) + (jax.ShapeDtypeStruct((8, own * n), f32),) * 2,
        in_specs=[anywhere] * 4 + [vmem] * 2 + [anywhere] * 2,
        out_specs=(anywhere,) * 4,
        scratch_shapes=[
            pltpu.VMEM((2, count, wide * 4), bf16),
            pltpu.VMEM((2, wt.shape[1] * n, own), bf16),
            pltpu.VMEM((wt.shape[1] * n, own), bf16),
            pltpu.VMEM((count, own), f32),
            pltpu.VMEM((rows, own * n), f32),
            pltpu.VMEM((rows, own * n), bf16),
            pltpu.VMEM((8, own * n), f32),
            pltpu.VMEM((count, own), bf16),
            pltpu.VMEM((n, 8, own), f32),
            pltpu.VMEM((2 * block, 3 * block), bf16),
            pltpu.VMEM((block, 6 * block), bf16),
            pltpu.VMEM((2 * count, own), f32),
            pltpu.VMEM((2 * count, own), f32),
            pltpu.VMEM((count, own), f32),
            pltpu.VMEM((count, own), f32),
            pltpu.VMEM((3 * block, own), bf16),
            pltpu.VMEM((blocks, 2 * block, own), f32),
            pltpu.VMEM((blocks // 2, 2 * block, own), f32),
            pltpu.VMEM((2, blocks, 2 * block, half), f32),
            pltpu.VMEM((6 * block, own), bf16),
            pltpu.VMEM((count, own), f32),
            pltpu.VMEM((2, rows, half), f32),
            pltpu.VMEM((2, 2, count, half), bf16),
            pltpu.VMEM((2, n, 2, 8, half), f32),
            sem((5,)), sem((8,)),
            sem((2, n, 2)), sem((2, n)), sem((2, n)), sem((2, n)), sem((2, 2, n)), sem((2, 2, n)),
            sem((6, n)), sem((6, n)), sem((6, n)), sem((6, n)), sem((n,)), sem((n,)), sem((n,)), sem((n,)),
            sem((n,)), sem((n,)),
            sem((2, 2, n)), sem((2, 2, n)), sem((2, 2)),
            sem((2, 2, n)), sem((2, 2, n)), sem((2, 2)),
        ],
        compiler_params=pltpu.CompilerParams(
            collective_id=0, has_side_effects=True, vmem_limit_bytes=60 * 2**20
        ),
        name="hyena",
    )(
        tokens, tangent, wt, long_filter, short_weight, skip_gain.reshape(1, -1),
        jnp.asarray(split_table(table, 1)), jnp.asarray(split_table(table.T, 1)),
    )
    return decode(first, unit0), decode(second, unit1)


def body(tokens, tangent, in_weight, short_weight, long_filter, skip_gain):
    devices = lax.axis_size("seq")
    shard = lax.axis_index("seq")
    own = in_weight.shape[2] // devices
    wt = in_weight.transpose(1, 0, 2)
    by_copies = own == 256 and devices == 4 and all(lax.axis_size(axis) == 2 for axis in ("grp", "chan", "sub"))
    block = min(512, long_filter.shape[0] * devices)
    if by_copies:
        return hyena(tokens, tangent, wt, long_filter, short_weight, skip_gain, block)

    both = jnp.stack([tokens, tangent])
    both = lax.all_gather(both, ("chan", "sub"), axis=2, tiled=True)
    both = lax.all_gather(both, "seq", axis=1, tiled=True)
    weight = lax.all_to_all(wt, "seq", split_axis=2, concat_axis=1, tiled=True)
    long_filter = lax.all_to_all(long_filter, "seq", split_axis=1, concat_axis=0, tiled=True)
    short_weight = lax.dynamic_slice_in_dim(short_weight, shard * own, own, axis=2)
    skip_gain = lax.dynamic_slice_in_dim(skip_gain, shard * own, own, axis=0)

    def project(values):
        return [jnp.dot(values, weight[j], preferred_element_type=jnp.float32) for j in range(3)]

    proj, dproj = project(both[0]), project(both[1])
    outs = operator(proj, dproj, short_weight, long_filter, skip_gain, block)
    return tuple(
        lax.all_to_all(value, "seq", split_axis=0, concat_axis=1, tiled=True) for value in outs
    )


def solution(mesh):
    placed = (
        P(("grp", "seq"), ("chan", "sub")),
        P(("grp", "seq"), ("chan", "sub")),
        P("seq", None, ("chan", "sub")),
        P(None, None, ("chan", "sub")),
        P("seq", ("chan", "sub")),
        P(("chan", "sub")),
    )
    return jax.shard_map(
        body,
        mesh=mesh,
        in_specs=placed,
        out_specs=(P(("grp", "seq"), ("chan", "sub")), P(("grp", "seq"), ("chan", "sub"))),
        check_vma=False,
    )
```

```python
import functools
import math

import jax
import jax.numpy as jnp
import numpy as np
from jax import lax
from jax.experimental import pallas as pl
from jax.experimental.pallas import tpu as pltpu
from jax.sharding import PartitionSpec as P

HIGH = lax.Precision.HIGH


def dft_table(block):
    size = 2 * block
    freqs = np.arange(block)[:, None]
    times = np.arange(block)[None, :]
    theta = (freqs * times % size) * (2.0 * math.pi / size)
    cosine = np.cos(theta)
    sine = -np.sin(theta)
    sine[0] = 1.0 - 2.0 * (np.arange(block) % 2)
    return np.concatenate([cosine, sine], axis=0).astype(np.float32)


def causal_convs(signals, long_filter, block):
    count = long_filter.shape[0]
    blocks = count // block
    table = jnp.asarray(dft_table(block))
    index = lax.broadcasted_iota(jnp.int32, (block, 1), 0)
    first = index == 0
    sign = (1 - 2 * (index % 2)).astype(jnp.float32)
    weight = jnp.where(first, 0.5 / block, 1.0 / block).astype(jnp.float32)

    def spectra(values):
        result = []
        for b in range(blocks):
            both = jnp.dot(table, values[b * block : (b + 1) * block], precision=HIGH)
            result.append((both[:block], both[block:]))
        return result

    plain = spectra(long_filter)
    kernels = [plain[0]]
    for b in range(1, blocks):
        kernels.append(tuple(here + sign * before for here, before in zip(plain[b], plain[b - 1])))
    outs = []
    for values in signals:
        moved = spectra(values)
        rows = []
        for b in range(blocks):
            real, imag = 0.0, 0.0
            for a in range(b + 1):
                kr, ki = kernels[b - a]
                vr, vi = moved[a]
                rr, ii = kr * vr, ki * vi
                real = real + jnp.where(first, rr, rr - ii)
                imag = imag + jnp.where(first, ii, kr * vi + ki * vr)
            packed = jnp.concatenate([real * weight, imag * weight], axis=0)
            rows.append(
                lax.dot_general(table, packed, (((0,), (0,)), ((), ())), precision=HIGH)
            )
        outs.append(jnp.concatenate(rows, axis=0))
    return outs


def short_filter(values, weights):
    count = values.shape[0]
    total = weights[0] * values
    for offset in range(1, weights.shape[0]):
        total = total + weights[offset] * jnp.pad(values, ((offset, 0), (0, 0)))[:count]
    return total


def operator(proj, dproj, short_weight, long_filter, skip_gain, block):
    mixed = [short_filter(proj[j], short_weight[:, j]) for j in range(3)]
    dmixed = [short_filter(dproj[j], short_weight[:, j]) for j in range(3)]
    gated_in = mixed[0] * mixed[2]
    dgated_in = dmixed[0] * mixed[2] + mixed[0] * dmixed[2]
    conv, dconv = causal_convs((gated_in, dgated_in), long_filter, block)
    combined = conv + skip_gain * gated_in
    dcombined = dconv + skip_gain * dgated_in
    return mixed[1] * combined, dmixed[1] * combined + mixed[1] * dcombined

MESH = pl.DeviceIdType.MESH
DIRECTIONS = (1, -1)


def split_table(table, axis):
    high = table.astype(jnp.bfloat16)
    low = (table - high.astype(np.float32)).astype(jnp.bfloat16)
    return np.concatenate([high, high, low], axis=axis)


def split_value(value):
    high = value.astype(jnp.bfloat16)
    return high, (value - high.astype(jnp.float32)).astype(jnp.bfloat16)


TILE = 256
STRIP = 64
POWER = 12
REACH = 1400.0
TINY = 1e-34


def encode(value):
    second = value * value
    fourth = second * second
    code = fourth * fourth * fourth
    return jnp.where(value < 0, -code, code).astype(jnp.bfloat16)


def decode(code, unit):
    value = code.astype(jnp.float32).reshape(-1, *unit.shape)
    size = jnp.exp2(jnp.log2(jnp.abs(value)) * (1.0 / POWER)) * unit
    return jnp.where(value > 0, size, jnp.where(value < 0, -size, 0.0)).reshape(code.shape)


def hyena_kernel(
    n, block, tok, tan, wt, filt, sw, skip, table_in, inverse_in, out0, out1, unit0, unit1,
    full, pairs, mid, ffull, fin, fown, uown, fcode, funit, table, inverse, p02, p1,
    gates, mids, xin, spec, plain, kern, ycat, conv, raw, res, top_of,
    local_sem, own_sem, col_send, col_recv, x_send, x_recv, c_send, c_recv,
    w_send, w_recv, y_send, y_recv, f_send, f_recv, fy_send, fy_recv, u_send, u_recv,
    send_sem, recv_sem, keep_sem, unit_send, unit_recv, unit_keep,
):
    g, z = lax.axis_index("grp"), lax.axis_index("seq")
    x, c = lax.axis_index("chan"), lax.axis_index("sub")
    rows, wide = tok.shape
    count = rows * n
    deep, own = wt.shape[1], wt.shape[2] // n
    half, deep2, fhalf = own // 2, deep // 2, filt.shape[0] // 2
    blocks = count // block
    taps = sw.shape[0]
    sources = (tok, tan)
    outs = (out0, out1)
    units = (unit0, unit1)
    pending = []

    def valid(place):
        return jnp.logical_and(place >= 0, place < n)

    def send(src, dst, send_sem, recv_sem, where):
        return pltpu.make_async_remote_copy(
            src_ref=src, dst_ref=dst, send_sem=send_sem, recv_sem=recv_sem,
            device_id=where, device_id_type=MESH,
        )

    def slot(k, zb, xb, cb):
        top = pl.multiple_of(zb * rows, rows)
        left = pl.multiple_of((xb * 2 + cb) * wide, wide)
        return full.at[k, pl.ds(top, rows), pl.ds(left, wide)]

    def column(k, zb, way, first):
        dst = slot(k, zb, x, c)
        src = sources[k] if first else dst
        lane = 0 if way > 0 else 1
        return send(src, dst, col_send.at[k, zb, lane], col_recv.at[k, zb], {"seq": z + way})

    def across(k, zb, first):
        dst = slot(k, zb, x, c)
        src = sources[k] if first else dst
        return send(src, dst, x_send.at[k, zb], x_recv.at[k, zb], {"chan": 1 - x})

    def sibling(k, zb, other, first):
        xb = 1 - x if other else x
        dst = slot(k, zb, xb, c)
        src = sources[k] if first else dst
        return send(src, dst, c_send.at[k, xb, zb], c_recv.at[k, xb, zb], {"sub": 1 - c})

    def from_sibling(k, zb, xb):
        dst = slot(k, zb, xb, 1 - c)
        return send(dst, dst, c_send.at[k, xb, zb], c_recv.at[k, xb, zb], {"sub": 1 - c})

    def from_across(k, zb):
        dst = slot(k, zb, 1 - x, c)
        return send(dst, dst, x_send.at[k, zb], x_recv.at[k, zb], {"chan": 1 - x})

    def weight_rows(piece, top, size):
        j, h = piece
        if j == 1:
            return mid.at[pl.ds(top, size), pl.ds(h * half, half)]
        return pairs.at[h, pl.ds(top, size), pl.ds((j // 2) * half, half)]

    def weight_part(piece, zb, gb):
        return weight_rows(piece, pl.multiple_of(zb * deep + gb * deep2, deep2), deep2)

    def filter_part(zb, gb):
        top = pl.multiple_of(zb * 2 * fhalf + gb * fhalf, fhalf)
        return fcode.at[pl.ds(top, fhalf), :]

    def number(piece):
        return piece[0] * 2 + piece[1]

    def give_weight(piece, target):
        left = pl.multiple_of(target * own + piece[1] * half, half)
        top = pl.multiple_of(g * deep2, deep2)
        src = wt.at[piece[0], pl.ds(top, deep2), pl.ds(left, half)]
        q = number(piece)
        return send(
            src, weight_part(piece, z, g), w_send.at[q, target], w_recv.at[q, z], {"seq": target}
        )

    def give_filter(target):
        left = pl.multiple_of(target * own, own)
        top = pl.multiple_of(g * fhalf, fhalf)
        src = fown.at[pl.ds(top, fhalf), pl.ds(left, own)]
        return send(src, filter_part(z, g), f_send.at[target], f_recv.at[z], {"seq": target})

    def give_scale(target):
        src = uown.at[:, pl.ds(pl.multiple_of(target * own, own), own)]
        return send(src, funit.at[z], u_send.at[target], u_recv.at[z], {"seq": target})

    def take_scale(zb):
        return send(funit.at[zb], funit.at[zb], u_send.at[zb], u_recv.at[zb], {"seq": zb})

    def take_weight(piece, zb):
        ref, q = weight_part(piece, zb, g), number(piece)
        return send(ref, ref, w_send.at[q, zb], w_recv.at[q, zb], {"seq": zb})

    def take_filter(zb):
        ref = filter_part(zb, g)
        return send(ref, ref, f_send.at[zb], f_recv.at[zb], {"seq": zb})

    def pass_weight(piece, zb):
        ref, q = weight_part(piece, zb, g), number(piece)
        return send(ref, ref, y_send.at[q, zb], y_recv.at[q, zb], {"grp": 1 - g})

    def pass_filter(zb):
        ref = filter_part(zb, g)
        return send(ref, ref, fy_send.at[zb], fy_recv.at[zb], {"grp": 1 - g})

    def end_weight(piece, zb):
        ref, q = weight_part(piece, zb, 1 - g), number(piece)
        return send(ref, ref, y_send.at[q, zb], y_recv.at[q, zb], {"grp": 1 - g})

    def end_filter(zb):
        ref = filter_part(zb, 1 - g)
        return send(ref, ref, fy_send.at[zb], fy_recv.at[zb], {"grp": 1 - g})

    barrier = pltpu.get_barrier_semaphore()
    for d in range(1, n):
        for way in DIRECTIONS:
            there = z + way * d

            @pl.when(valid(there))
            def _():
                pl.semaphore_signal(barrier, inc=1, device_id={"seq": there}, device_id_type=MESH)

    for where in ({"chan": 1 - x}, {"grp": 1 - g}, {"sub": 1 - c}):
        pl.semaphore_signal(barrier, inc=1, device_id=where, device_id_type=MESH)
    pl.semaphore_wait(barrier, n + 2)

    def launch(make, condition=None):
        pending.append((make, condition))
        if condition is None:
            make().start()
        else:
            pl.when(condition)(lambda: make().start())

    for k in range(2):
        for way in DIRECTIONS:
            launch(functools.partial(column, k, z, way, True), valid(z + way))
        launch(functools.partial(across, k, z, True))
        launch(functools.partial(sibling, k, z, False, True))
    mine = pl.ds(pl.multiple_of(z * own, own), own)
    locals_ = [
        pltpu.make_async_copy(tok, slot(0, z, x, c), local_sem.at[0]),
        pltpu.make_async_copy(tan, slot(1, z, x, c), local_sem.at[1]),
        pltpu.make_async_copy(table_in, table, local_sem.at[3]),
        pltpu.make_async_copy(inverse_in, inverse, local_sem.at[4]),
    ]
    for j in range(3):
        for h in range(2):
            piece = (j, h)
            left = pl.multiple_of(z * own + h * half, half)
            locals_.append(
                pltpu.make_async_copy(
                    wt.at[j, :, pl.ds(left, half)],
                    weight_rows(piece, pl.multiple_of(z * deep, deep), deep),
                    own_sem.at[number(piece)],
                )
            )
    for copy in locals_:
        copy.start()
    fetch = pltpu.make_async_copy(filt, fin, local_sem.at[2])
    fetch.start()
    fetch.wait()

    def highest(m, most):
        at = pl.ds(pl.multiple_of(m * STRIP, STRIP), STRIP)
        size = jnp.abs(fin[at, :]).reshape(STRIP // 8, 8, own * n)
        return jnp.maximum(most, jnp.max(size, axis=0))

    most = lax.fori_loop(0, 2 * fhalf // STRIP, highest, jnp.zeros((8, own * n), jnp.float32))
    peak = jnp.maximum(jnp.max(most, axis=0, keepdims=True), TINY)
    uown[...] = jnp.broadcast_to(peak * (1.0 / REACH), (8, own * n))
    scale = REACH / peak

    @pl.loop(0, 2 * fhalf // STRIP)
    def _(m):
        at = pl.ds(pl.multiple_of(m * STRIP, STRIP), STRIP)
        fown[at, :] = encode(fin[at, :] * scale)

    own_filter = [
        pltpu.make_async_copy(
            fown.at[:, mine],
            fcode.at[pl.ds(pl.multiple_of(z * 2 * fhalf, 2 * fhalf), 2 * fhalf), :],
            own_sem.at[6],
        ),
        pltpu.make_async_copy(uown.at[:, mine], funit.at[z], own_sem.at[7]),
    ]
    for copy in own_filter:
        copy.start()
    locals_ = locals_ + own_filter

    def relay_across(d):
        for k in range(2):
            for way in DIRECTIONS[: 1 if d == 0 else 2]:
                zb = z - way * d

                def step(k=k, zb=zb):
                    from_across(k, zb).wait_recv()
                    sibling(k, zb, True, False).start()

                pending.append((functools.partial(sibling, k, zb, True, False), valid(zb)))
                pl.when(valid(zb))(step)

    def relay_column(d):
        for k in range(2):
            for way in DIRECTIONS:
                zb = z - way * d
                on = jnp.logical_and(valid(zb), valid(z + way))

                def arrive(k=k, zb=zb, way=way):
                    column(k, zb, way, False).wait_recv()

                def after(k=k, zb=zb):
                    across(k, zb, False).start()
                    sibling(k, zb, False, False).start()

                pl.when(valid(zb))(arrive)
                launch(functools.partial(column, k, zb, way, False), on)
                pl.when(valid(zb))(after)
                pending.append((functools.partial(across, k, zb, False), valid(zb)))
                pending.append((functools.partial(sibling, k, zb, False, False), valid(zb)))

    def issue(make):
        for d in range(1, n):
            for way in DIRECTIONS:
                launch(functools.partial(make, z + way * d), valid(z + way * d))

    def each_source(step):
        for d in range(1, n):
            for way in DIRECTIONS:
                pl.when(valid(z - way * d))(functools.partial(step, z - way * d))

    def relay(take, give_on):
        def move(zb):
            take(zb).wait_recv()
            give_on(zb).start()

        each_source(move)
        for d in range(1, n):
            for way in DIRECTIONS:
                pending.append((functools.partial(give_on, z - way * d), valid(z - way * d)))

    def issue_weight(piece):
        issue(functools.partial(give_weight, piece))

    def relay_weight(piece):
        relay(functools.partial(take_weight, piece), functools.partial(pass_weight, piece))

    def finish_weight(piece):
        each_source(lambda zb: end_weight(piece, zb).wait_recv())

    def finish_tokens(d):
        for way in DIRECTIONS[: 1 if d == 0 else 2]:
            zb = z - way * d

            def finish(zb=zb):
                for k in range(2):
                    for xb in (x, 1 - x):
                        from_sibling(k, zb, xb).wait_recv()

            pl.when(valid(zb))(finish)

    def multiply_pair(h, zb):
        @pl.loop(0, 2)
        def _(k):
            top = pl.multiple_of(zb * rows, rows)
            to = pl.multiple_of(k * count + zb * rows, rows)
            p02[pl.ds(to, rows), :] = jnp.dot(
                full[k, pl.ds(top, rows), :], pairs[h], preferred_element_type=jnp.float32
            )

    def near(multiply, h, d):
        for way in DIRECTIONS[: 1 if d == 0 else 2]:
            pl.when(valid(z - way * d))(functools.partial(multiply, h, z - way * d))

    def multiply_rows(zb):
        @pl.loop(0, 2)
        def _(k):
            top = pl.multiple_of(zb * rows, rows)
            to = pl.multiple_of(k * count + zb * rows, rows)
            p1[pl.ds(to, rows), :] = jnp.dot(
                full[k, pl.ds(top, rows), :], mid[...], preferred_element_type=jnp.float32
            )

    def multiply_slice(h, zs, first):
        depth = pl.ds(pl.multiple_of(zs * deep, deep), deep)

        @pl.loop(0, 2 * n)
        def _(i):
            top = pl.multiple_of((i % n) * rows, rows)
            to = pl.ds(pl.multiple_of(i * rows, rows), rows)
            part = jnp.dot(
                full[i // n, pl.ds(top, rows), depth], pairs[h, depth, :],
                preferred_element_type=jnp.float32,
            )
            p02[to, :] = part if first else p02[to, :] + part

    line = lax.broadcasted_iota(jnp.int32, (count, half), 0)

    def forward(value, dst):
        high, low = split_value(value)
        xin[pl.ds(0, block), :] = high
        xin[pl.ds(block, block), :] = low
        xin[pl.ds(2 * block, block), :] = high

        @pl.loop(0, 2 * block // TILE)
        def _(m):
            at = pl.ds(pl.multiple_of(m * TILE, TILE), TILE)
            dst[at, :] = jnp.dot(table[at, :], xin[...], preferred_element_type=jnp.float32)

    def filter_spectra(h):
        lanes = pl.ds(h * half, half)
        for pair in range(blocks // 2):
            forward(
                jnp.concatenate(
                    [
                        ffull[pl.ds(2 * pair * block, block), lanes],
                        ffull[pl.ds((2 * pair + 1) * block, block), lanes],
                    ],
                    axis=1,
                ),
                plain.at[pair],
            )

        @pl.loop(0, 2 * block // STRIP)
        def _(m):
            at = pl.ds(pl.multiple_of(m * STRIP, STRIP), STRIP)
            row = lax.broadcasted_iota(jnp.int32, (STRIP, half), 0)
            sign = (1 - 2 * (row % 2)).astype(jnp.float32)
            before = None
            for b in range(blocks):
                left = (b % 2) * half
                here = plain[b // 2, at, left : left + half]
                kern[h, b, at, :] = here if before is None else here + sign * before
                before = here

    def filtered(ref, lanes, j, h, s):
        own_lanes = pl.ds(pl.multiple_of(z * own + h * half, half), half)
        value = ref[pl.ds(s * count, count), lanes]
        total = sw[0, pl.ds(j, 1), own_lanes] * value
        for o in range(1, taps):
            moved = jnp.where(line >= o, pltpu.roll(value, o, 0), 0.0)
            total = total + sw[o, pl.ds(j, 1), own_lanes] * moved
        return total

    def transform(h):
        low_lanes, high_lanes = pl.ds(0, half), pl.ds(half, half)
        first_gate = filtered(p02, low_lanes, 0, h, 0)
        second_gate = filtered(p02, high_lanes, 2, h, 0)
        gates[:, :half] = first_gate * second_gate
        gates[:, half:] = filtered(p02, low_lanes, 0, h, 1) * second_gate + first_gate * filtered(
            p02, high_lanes, 2, h, 1
        )
        for b in range(blocks):
            forward(gates[pl.ds(b * block, block), :], spec.at[b])

    def convolve(h):
        for b in range(blocks):

            @pl.loop(0, block // STRIP)
            def _(m):
                at = pl.ds(pl.multiple_of(m * STRIP, STRIP), STRIP)
                after = pl.ds(pl.multiple_of(block + m * STRIP, STRIP), STRIP)
                row = lax.broadcasted_iota(jnp.int32, (STRIP, 2 * half), 0) + m * STRIP
                first = row == 0
                weight = jnp.where(first, 0.5 / block, 1.0 / block)
                real, imag = 0.0, 0.0
                for a in range(b + 1):
                    kr, ki = kern[h, b - a, at, :], kern[h, b - a, after, :]
                    kr, ki = jnp.concatenate([kr, kr], axis=1), jnp.concatenate([ki, ki], axis=1)
                    vr, vi = spec[a, at, :], spec[a, after, :]
                    rr, ii = kr * vr, ki * vi
                    real = real + jnp.where(first, rr, rr - ii)
                    imag = imag + jnp.where(first, ii, kr * vi + ki * vr)
                for base, value in ((0, real), (block, imag)):
                    high, low = split_value(value * weight)
                    for third, part in enumerate((high, low, high)):
                        start = pl.multiple_of(third * 2 * block + base + m * STRIP, STRIP)
                        ycat[pl.ds(start, STRIP), :] = part

            @pl.loop(0, block // TILE)
            def _(m):
                at = pl.ds(pl.multiple_of(m * TILE, TILE), TILE)
                to = pl.ds(pl.multiple_of(b * block + m * TILE, TILE), TILE)
                conv[to, :] = jnp.dot(
                    inverse[at, :], ycat[...], preferred_element_type=jnp.float32
                )

    def give(h, o, target):
        top = pl.multiple_of(target * rows, rows)
        left = pl.multiple_of(z * own + h * half, half)
        return send(
            res.at[h, o, pl.ds(top, rows), :], outs[o].at[:, pl.ds(left, half)],
            send_sem.at[h, o, target], recv_sem.at[h, o, z], {"seq": target},
        )

    def take(h, o, source):
        top = pl.multiple_of(source * rows, rows)
        left = pl.multiple_of(source * own + h * half, half)
        return send(
            res.at[h, o, pl.ds(top, rows), :], outs[o].at[:, pl.ds(left, half)],
            send_sem.at[h, o, source], recv_sem.at[h, o, source], {"seq": source},
        )

    def keep(h, o):
        top = pl.multiple_of(z * rows, rows)
        left = pl.multiple_of(z * own + h * half, half)
        return pltpu.make_async_copy(
            res.at[h, o, pl.ds(top, rows), :], outs[o].at[:, pl.ds(left, half)], keep_sem.at[h, o]
        )

    def unit_place(h, o, source):
        left = pl.multiple_of(source * own + h * half, half)
        return units[o].at[:, pl.ds(left, half)]

    def give_unit(h, o, target):
        return send(
            top_of.at[h, target, o], unit_place(h, o, z),
            unit_send.at[h, o, target], unit_recv.at[h, o, z], {"seq": target},
        )

    def take_unit(h, o, source):
        return send(
            top_of.at[h, source, o], unit_place(h, o, source),
            unit_send.at[h, o, source], unit_recv.at[h, o, source], {"seq": source},
        )

    def keep_unit(h, o):
        return pltpu.make_async_copy(
            top_of.at[h, z, o], unit_place(h, o, z), unit_keep.at[h, o]
        )

    def prepare(h):
        mids[:, :half] = filtered(p1, pl.ds(h * half, half), 1, h, 0)
        mids[:, half:] = filtered(p1, pl.ds(h * half, half), 1, h, 1)

    def answer(h):
        gain = skip[:, pl.ds(pl.multiple_of(z * own + h * half, half), half)]

        @pl.loop(0, n)
        def _(i):
            target = jnp.where(z < n // 2, n - 1 - i, i)

            def values(m, most):
                at = pl.ds(pl.multiple_of(target * rows + m * STRIP, STRIP), STRIP)
                combined = conv[at, :half] + gain * gates[at, :half]
                dcombined = conv[at, half:] + gain * gates[at, half:]
                middle = mids[at, :half]
                first = middle * combined
                second = mids[at, half:] * combined + middle * dcombined
                here = pl.ds(pl.multiple_of(m * STRIP, STRIP), STRIP)
                raw[0, here, :] = first
                raw[1, here, :] = second
                return tuple(
                    jnp.maximum(old, jnp.max(jnp.abs(new).reshape(STRIP // 8, 8, half), axis=0))
                    for old, new in zip(most, (first, second))
                )

            nothing = jnp.zeros((8, half), jnp.float32)
            most = lax.fori_loop(0, rows // STRIP, values, (nothing, nothing))
            for o in range(2):
                peak = jnp.maximum(jnp.max(most[o], axis=0, keepdims=True), TINY)
                top_of[h, target, o] = jnp.broadcast_to(peak * (1.0 / REACH), (8, half))
                scale = REACH / peak

                @pl.loop(0, rows // STRIP)
                def _(m):
                    here = pl.ds(pl.multiple_of(m * STRIP, STRIP), STRIP)
                    at = pl.ds(pl.multiple_of(target * rows + m * STRIP, STRIP), STRIP)
                    res[h, o, at, :] = encode(raw[o, here, :] * scale)

            @pl.when(target != z)
            def _():
                for o in range(2):
                    give_unit(h, o, target).start()
                    give(h, o, target).start()

        for o in range(2):
            keep_unit(h, o).start()
            keep(h, o).start()

    def issue_filter():
        issue(give_scale)
        issue(give_filter)

    def relay_filter():
        relay(take_filter, pass_filter)

    first_pair, second_pair = ((0, 0), (2, 0)), ((0, 1), (2, 1))
    first_mid, second_mid = (1, 0), (1, 1)

    relay_column(1)
    issue_filter()
    for piece in (*first_pair, first_mid):
        issue_weight(piece)
    relay_across(0)
    relay_column(2)
    relay_across(1)
    relay_filter()
    relay_weight(first_pair[0])
    issue_weight(second_mid)
    relay_weight(first_pair[1])
    relay_weight(first_mid)
    issue_weight(second_pair[0])
    for d in range(3, n):
        relay_column(d)
    relay_across(2)
    for copy in locals_:
        copy.wait()
    each_source(lambda zb: end_filter(zb).wait_recv())
    each_source(lambda zb: take_scale(zb).wait_recv())

    @pl.loop(0, count // STRIP)
    def _(m):
        at = pl.ds(pl.multiple_of(m * STRIP, STRIP), STRIP)
        ffull[at, :] = decode(fcode[at, :], funit[m // (2 * fhalf // STRIP)])

    for h in range(2):
        filter_spectra(h)
    for piece in first_pair:
        finish_weight(piece)
    for d in range(2):
        finish_tokens(d)
        near(multiply_pair, 0, d)
    relay_weight(second_mid)
    issue_weight(second_pair[1])
    finish_tokens(2)
    near(multiply_pair, 0, 2)
    relay_weight(second_pair[0])
    for d in range(3, n):
        relay_across(d)
        finish_tokens(d)
        near(multiply_pair, 0, d)
    transform(0)
    convolve(0)
    relay_weight(second_pair[1])
    finish_weight(first_mid)
    finish_weight(second_mid)

    @pl.loop(0, n)
    def _(zb):
        multiply_rows(zb)

    prepare(0)
    answer(0)
    prepare(1)
    finish_weight(second_pair[0])
    multiply_slice(1, z, True)

    def source(i):
        return jnp.where(z < n // 2, lax.rem(z + i, n), lax.rem(z + n - i, n))

    for i in range(1, n):
        end_weight(second_pair[1], source(i)).wait_recv()
        multiply_slice(1, source(i), False)
    transform(1)
    convolve(1)
    answer(1)

    for make, condition in pending:
        if condition is None:
            make().wait_send()
        else:
            pl.when(condition)(lambda make=make: make().wait_send())
    for h in range(2):
        for o in range(2):
            keep_unit(h, o).wait()
            keep(h, o).wait()
        for d in range(1, n):
            for way in DIRECTIONS:
                there = z + way * d

                def finish(h=h, there=there):
                    for o in range(2):
                        take_unit(h, o, there).wait_recv()
                        give_unit(h, o, there).wait_send()
                        take(h, o, there).wait_recv()
                        give(h, o, there).wait_send()

                pl.when(valid(there))(finish)


def hyena(tokens, tangent, wt, long_filter, short_weight, skip_gain, block):
    n = lax.axis_size("seq")
    rows, wide = tokens.shape
    own = wt.shape[2] // n
    half, count = own // 2, rows * n
    blocks = count // block
    table = dft_table(block)
    vmem = pl.BlockSpec(memory_space=pltpu.VMEM)
    anywhere = pl.BlockSpec(memory_space=pl.ANY)
    sem = pltpu.SemaphoreType.DMA
    f32, bf16 = jnp.float32, jnp.bfloat16
    shape = jax.ShapeDtypeStruct((rows, own * n), bf16)
    first, second, unit0, unit1 = pl.pallas_call(
        functools.partial(hyena_kernel, n, block),
        out_shape=(shape, shape) + (jax.ShapeDtypeStruct((8, own * n), f32),) * 2,
        in_specs=[anywhere] * 4 + [vmem] * 2 + [anywhere] * 2,
        out_specs=(anywhere,) * 4,
        scratch_shapes=[
            pltpu.VMEM((2, count, wide * 4), bf16),
            pltpu.VMEM((2, wt.shape[1] * n, own), bf16),
            pltpu.VMEM((wt.shape[1] * n, own), bf16),
            pltpu.VMEM((count, own), f32),
            pltpu.VMEM((rows, own * n), f32),
            pltpu.VMEM((rows, own * n), bf16),
            pltpu.VMEM((8, own * n), f32),
            pltpu.VMEM((count, own), bf16),
            pltpu.VMEM((n, 8, own), f32),
            pltpu.VMEM((2 * block, 3 * block), bf16),
            pltpu.VMEM((block, 6 * block), bf16),
            pltpu.VMEM((2 * count, own), f32),
            pltpu.VMEM((2 * count, own), f32),
            pltpu.VMEM((count, own), f32),
            pltpu.VMEM((count, own), f32),
            pltpu.VMEM((3 * block, own), bf16),
            pltpu.VMEM((blocks, 2 * block, own), f32),
            pltpu.VMEM((blocks // 2, 2 * block, own), f32),
            pltpu.VMEM((2, blocks, 2 * block, half), f32),
            pltpu.VMEM((6 * block, own), bf16),
            pltpu.VMEM((count, own), f32),
            pltpu.VMEM((2, rows, half), f32),
            pltpu.VMEM((2, 2, count, half), bf16),
            pltpu.VMEM((2, n, 2, 8, half), f32),
            sem((5,)), sem((8,)),
            sem((2, n, 2)), sem((2, n)), sem((2, n)), sem((2, n)), sem((2, 2, n)), sem((2, 2, n)),
            sem((6, n)), sem((6, n)), sem((6, n)), sem((6, n)), sem((n,)), sem((n,)), sem((n,)), sem((n,)),
            sem((n,)), sem((n,)),
            sem((2, 2, n)), sem((2, 2, n)), sem((2, 2)),
            sem((2, 2, n)), sem((2, 2, n)), sem((2, 2)),
        ],
        compiler_params=pltpu.CompilerParams(
            collective_id=0, has_side_effects=True, vmem_limit_bytes=60 * 2**20
        ),
        name="hyena",
    )(
        tokens, tangent, wt, long_filter, short_weight, skip_gain.reshape(1, -1),
        jnp.asarray(split_table(table, 1)), jnp.asarray(split_table(table.T, 1)),
    )
    return decode(first, unit0), decode(second, unit1)


def body(tokens, tangent, in_weight, short_weight, long_filter, skip_gain):
    devices = lax.axis_size("seq")
    shard = lax.axis_index("seq")
    own = in_weight.shape[2] // devices
    wt = in_weight.transpose(1, 0, 2)
    by_copies = own == 256 and devices == 4 and all(lax.axis_size(axis) == 2 for axis in ("grp", "chan", "sub"))
    block = min(512, long_filter.shape[0] * devices)
    if by_copies:
        return hyena(tokens, tangent, wt, long_filter, short_weight, skip_gain, block)

    both = jnp.stack([tokens, tangent])
    both = lax.all_gather(both, ("chan", "sub"), axis=2, tiled=True)
    both = lax.all_gather(both, "seq", axis=1, tiled=True)
    weight = lax.all_to_all(wt, "seq", split_axis=2, concat_axis=1, tiled=True)
    long_filter = lax.all_to_all(long_filter, "seq", split_axis=1, concat_axis=0, tiled=True)
    short_weight = lax.dynamic_slice_in_dim(short_weight, shard * own, own, axis=2)
    skip_gain = lax.dynamic_slice_in_dim(skip_gain, shard * own, own, axis=0)

    def project(values):
        return [jnp.dot(values, weight[j], preferred_element_type=jnp.float32) for j in range(3)]

    proj, dproj = project(both[0]), project(both[1])
    outs = operator(proj, dproj, short_weight, long_filter, skip_gain, block)
    return tuple(
        lax.all_to_all(value, "seq", split_axis=0, concat_axis=1, tiled=True) for value in outs
    )


def solution(mesh):
    placed = (
        P(("grp", "seq"), ("chan", "sub")),
        P(("grp", "seq"), ("chan", "sub")),
        P("seq", None, ("chan", "sub")),
        P(None, None, ("chan", "sub")),
        P("seq", ("chan", "sub")),
        P(("chan", "sub")),
    )
    return jax.shard_map(
        body,
        mesh=mesh,
        in_specs=placed,
        out_specs=(P(("grp", "seq"), ("chan", "sub")), P(("grp", "seq"), ("chan", "sub"))),
        check_vma=False,
    )
```
